512 devices in a mesh: row: 16 (over z), col: 32 (over y, x, core).
Axes of the slice: x: 4, y: 4, z: 16, core: 2. Of those that a mesh axis runs over, the one named last changes fastest.
Arguments:
- ancestor_inverse: float32 [16384, 16384], P('row', 'col'), may hold values from -6 to 6
- panel_one: bfloat16 [16384, 256], P(('row', 'col')), may hold values from -0.046875 to 0.046875
- panel_two: bfloat16 [16384, 256], P(('row', 'col')), may hold values from -0.046875 to 0.046875
- panel_three: bfloat16 [16384, 256], P(('row', 'col')), may hold values from -0.046875 to 0.046875
- couplings: bfloat16 [3, 256, 256], replicated, may hold values from -0.375 to 0.375
- diag_terms: float32 [3, 256, 256], replicated, may hold values from -6 to 6
- list_two: int32 [60], replicated, may hold values from 0 to 63, as said below
- list_three: int32 [56], replicated, may hold values from 0 to 63, as said below
Outputs:
- inverse_one: float32 [16384, 256], P(('row', 'col'))
- inverse_two: float32 [16384, 256], P(('row', 'col'))
- inverse_three: float32 [16384, 256], P(('row', 'col'))
- small_blocks: float32 [6, 256, 256], P(None, 'row', 'col')
The draws below stay inside these ranges and needn't reach their ends.
Inputs may be any that keep to these rules, and one draw needn't show every extreme that they name: `list_two`: 60 distinct block indices in increasing order, always including 0 and 63. `list_three`: 56 distinct entries of list_two in increasing order, always including 0 and 63.
All inputs are finite; a program needn't handle non-finite values.
Results may differ from the reference program's by a relative error of at most 0.0003.
Values may be sent and summed in bfloat16 or wider, within the bound.
A program may use at most 64 MiB of HBM per device.

```python
import jax
import jax.numpy as jnp
from jax import lax

W = 256
NB = 64
B2 = 60
B3 = 56
R = 16384


def pick_lists(key):
    inner_ids = 1 + jax.random.permutation(jax.random.fold_in(key, 7101), NB - 2).astype(jnp.int32)
    chosen = inner_ids[:B2 - 2]
    first_block = jnp.zeros((1,), jnp.int32)
    last_block = jnp.full((1,), NB - 1, jnp.int32)
    listed_two = jnp.sort(jnp.concatenate([first_block, chosen, last_block]))
    shuffled = jax.random.permutation(jax.random.fold_in(key, 7102), B2 - 2).astype(jnp.int32)
    kept_ids = chosen[shuffled[:B3 - 2]]
    listed_three = jnp.sort(jnp.concatenate([first_block, kept_ids, last_block]))
    return (listed_two, listed_three)


def draw_list_two(key, part):
    return pick_lists(key)[0]


def draw_list_three(key, part):
    return pick_lists(key)[1]


def raised(drawn, own_key, source, target, shards_of, factor):
    owner, partner = [(jnp.arange(drawn.shape[dim]) // (drawn.shape[dim] // shards_of)).reshape([-1 if axis == dim else 1 for axis in range(drawn.ndim)]) for dim in (source, target)]
    chosen = jax.random.permutation(own_key, shards_of)[partner]
    strong = (owner == chosen) | (owner == (partner + shards_of // 2) % shards_of)
    return jnp.where(strong, factor * drawn, drawn)


def shard_levels(key, dims, split, smallest, high):
    level, own = 1.0, jax.random.fold_in(key, 6)
    for dim, parts in split:
        draws = jnp.exp(jax.random.uniform(jax.random.fold_in(own, dim), (parts,), jnp.float32, smallest / len(split), high / len(split)))
        level = level * jnp.repeat(draws, dims[dim] // parts).reshape([-1 if axis == dim else 1 for axis in range(len(dims))])
    return level


def centred(stream_key, shape, width, bound, pieces=(), kind=jnp.bfloat16):
    array = width * jax.random.normal(stream_key, shape, jnp.float32)
    if pieces:
        array = array * shard_levels(stream_key, shape, pieces, -0.22, 0.18)
    return jnp.clip(array, -bound, bound).astype(kind)


def gaussian_with(rng, dims, spread, bound, pieces, heavy, kind=jnp.bfloat16):
    entries = spread * jax.random.normal(rng, dims, jnp.float32)
    if pieces:
        entries = entries * shard_levels(rng, dims, pieces, -0.22, 0.18)
    return jnp.clip(raised(entries, jax.random.fold_in(rng, 3), *heavy), -bound, bound).astype(kind)


def setup_inputs(seed: int = 0) -> dict:
    arg_keys = jax.random.split(jax.random.key(seed), 9)
    return {
        "ancestor_inverse": gaussian_with(arg_keys[0], (R, R), 1.0, 6.0, ((0, 16), (1, 32)), (1, 0, 32, 2.75), jnp.float32),
        "panel_one": centred(arg_keys[1], (R, W), (NB * W) ** -0.5, 0.046875, ((0, 512),)),
        "panel_two": centred(arg_keys[2], (R, W), (NB * W) ** -0.5, 0.046875, ((0, 512),)),
        "panel_three": centred(arg_keys[3], (R, W), (NB * W) ** -0.5, 0.046875, ((0, 512),)),
        "couplings": centred(arg_keys[4], (3, W, W), W ** -0.5, 0.375),
        "diag_terms": centred(arg_keys[5], (3, W, W), 1.0, 6.0, (), jnp.float32),
        "list_two": draw_list_two(jax.random.fold_in(arg_keys[8], 71), 0),
        "list_three": draw_list_three(jax.random.fold_in(arg_keys[8], 71), 0),
    }


def product(former, latter):
    return jnp.dot(former, latter, precision=lax.Precision.HIGHEST, preferred_element_type=jnp.float32)


def inner_product(former, latter):
    return lax.dot_general(former, latter, (((0,), (0,)), ((), ())), precision=lax.Precision.HIGHEST, preferred_element_type=jnp.float32)


def row_keep(listed):
    blocks = jnp.arange(NB * W, dtype=jnp.int32) // W
    matches = blocks[:, None] == listed[None, :].astype(jnp.int32)
    return jnp.any(matches, axis=1).astype(jnp.float32)[:, None]


def reference(ancestor_inverse, panel_one, panel_two, panel_three, couplings, diag_terms, list_two, list_three):
    keep_two = row_keep(list_two)
    keep_three = row_keep(list_three)
    factor_one = panel_one.astype(jnp.float32)
    factor_two = panel_two.astype(jnp.float32) * keep_two
    factor_three = panel_three.astype(jnp.float32) * keep_three
    coupled = couplings.astype(jnp.float32)
    inverse_one = -product(ancestor_inverse, factor_one)
    diag_one = diag_terms[0] - inner_product(factor_one, inverse_one)
    inverse_two = -(product(ancestor_inverse, factor_two) + product(inverse_one, coupled[0])) * keep_two
    cross_two = -(inner_product(inverse_one, factor_two) + product(diag_one, coupled[0]))
    diag_two = diag_terms[1] - inner_product(factor_two, inverse_two) - inner_product(coupled[0], cross_two)
    inverse_three = -(product(ancestor_inverse, factor_three) + product(inverse_one, coupled[1]) + product(inverse_two, coupled[2])) * keep_three
    cross_first = -(inner_product(inverse_one, factor_three) + product(diag_one, coupled[1]) + product(cross_two, coupled[2]))
    cross_second = -(inner_product(inverse_two, factor_three) + inner_product(cross_two, coupled[1]) + product(diag_two, coupled[2]))
    diag_three = diag_terms[2] - inner_product(factor_three, inverse_three) - inner_product(coupled[1], cross_first) - inner_product(coupled[2], cross_second)
    stacked = jnp.stack([diag_one, diag_two, diag_three, cross_two, cross_first, cross_second])
    return inverse_one, inverse_two, inverse_three, stacked
```

```python
import functools

import jax
import jax.numpy as jnp
from jax import lax
from jax.experimental import pallas as pl
from jax.experimental.pallas import tpu as pltpu
from jax.sharding import PartitionSpec as P

MESH = pl.DeviceIdType.MESH
HI = lax.Precision.HIGHEST
F32 = jnp.float32
BF16 = jnp.bfloat16
NZ, NK, W, ROWS = 16, 16, 256, 32
HALF = 384


def mm(a, b):
    return jnp.dot(a, b, precision=HI, preferred_element_type=F32)


def tmm(a, b):
    return lax.dot_general(a, b, (((0,), (0,)), ((), ())), precision=HI, preferred_element_type=F32)


def keep_of(lines, block):
    return jnp.max(jnp.where(lines == block, 1.0, 0.0).astype(F32))


def kernel(
    a_hbm, p1, p2, p3, coup, diag, l2, l3,
    o1, o2, o3, ot,
    a_vm, ahi, alo, ring, fbuf, pown, ppar, prec,
    xra, yra, xrb, yrb, ra, rb, ysum,
    phi, qrec, x2a, y2a, x2b, y2b, r2a, r2b, zsend, zrec,
    lsem, up_s, up_r, dn_s, dn_r, f_s, f_r, pr_s, pr_r,
    xa_s, xa_r, ya_s, ya_r, xb_s, xb_r, yb_s, yb_r,
    q_s, q_r, x2a_s, x2a_r, y2a_s, y2a_r, x2b_s, x2b_r, y2b_s, y2b_r, z_s, z_r,
):
    z = lax.axis_index("row")
    c = lax.axis_index("col")
    e = c % 2
    k = c // 2
    y = k // 4
    x = k % 4
    half = y // 2
    partner = k * 2 + (1 - e)

    def col_of(yy, xx):
        return (yy * 4 + xx) * 2 + e

    acopy = pltpu.make_async_copy(a_hbm, a_vm, lsem.at[0])
    acopy.start()
    own = []
    for i, p in enumerate((p1, p2, p3)):
        cp = pltpu.make_async_copy(p, ring.at[z, :, pl.ds(i * W, W)], lsem.at[1 + i])
        cp.start()
        own.append(cp)

    barrier = pltpu.get_barrier_semaphore()
    for d in range(1, 32):
        pl.semaphore_signal(barrier, inc=1, device_id=(z, (c + d) % 32), device_id_type=MESH)
    for d in range(1, 16):
        pl.semaphore_signal(barrier, inc=1, device_id=((z + d) % 16, c), device_id_type=MESH)

    lines2 = l2[...]
    lines3 = l3[...]
    block = (z * 32 + c) // 8
    keep2 = keep_of(lines2, block)
    keep3 = keep_of(lines3, block)
    c0 = coup[0].astype(F32)
    c1 = coup[1].astype(F32)
    c2 = coup[2].astype(F32)
    first = jnp.where((z == 0) & (c == 0), 1.0, 0.0).astype(F32)
    g1 = diag[0]
    h21 = -mm(g1, c0)
    g2 = diag[1] - tmm(c0, h21)
    h31 = -(mm(g1, c1) + mm(h21, c2))
    h32 = -(tmm(h21, c1) + mm(g2, c2))
    g3 = diag[2] - tmm(c1, h31) - tmm(c2, h32)
    for i, v in enumerate((g1, g2, g3, h21, h31, h32)):
        phi[i] = (v.T * first).reshape(4, 4, 2, 8, W)

    acopy.wait()

    @pl.loop(0, 16)
    def _(i):
        v = a_vm[pl.ds(pl.multiple_of(i * 64, 64), 64), :]
        hi = v.astype(BF16)
        ahi[i] = hi.reshape(2, 32, 512)
        alo[i] = (v - hi.astype(F32)).astype(BF16).reshape(2, 32, 512)

    for cp in own:
        cp.wait()
    pl.semaphore_wait(barrier, 46)

    up, down = (z + 1) % 16, (z + 15) % 16
    slot = (k % 8) * 2 + e

    def ring_copy(item, s, send, recv, to):
        return pltpu.make_async_remote_copy(
            src_ref=ring.at[item], dst_ref=ring.at[item], send_sem=send.at[s], recv_sem=recv.at[s],
            device_id=(to, c), device_id_type=MESH)

    def plane_copy(item):
        return pltpu.make_async_remote_copy(
            src_ref=ring.at[item], dst_ref=fbuf.at[slot], send_sem=f_s.at[item], recv_sem=f_r.at[slot],
            device_id=(z, item * 2 + half), device_id_type=MESH)

    def spread(item):
        mine = (item * 2 + half) == c

        @pl.when(mine)
        def _():
            pltpu.make_async_copy(ring.at[item], fbuf.at[slot], f_r.at[slot]).start()

        @pl.when(jnp.logical_not(mine))
        def _():
            plane_copy(item).start()

    ring_copy(z, 0, up_s, up_r, up).start()
    ring_copy(z, 0, dn_s, dn_r, down).start()
    spread(z)
    for s in range(1, 9):
        item = (z + 16 - s) % 16
        ring_copy(item, s - 1, up_s, up_r, up).wait_recv()
        if s < 8:
            ring_copy(item, s, up_s, up_r, up).start()
        spread(item)
        if s < 8:
            item = (z + s) % 16
            ring_copy(item, s - 1, dn_s, dn_r, down).wait_recv()
            if s < 7:
                ring_copy(item, s, dn_s, dn_r, down).start()
            spread(item)

    f1 = ring[z, :, 0:W].astype(F32)
    f2 = ring[z, :, W:2 * W].astype(F32) * keep2
    f3 = ring[z, :, 2 * W:3 * W].astype(F32) * keep3
    b = mm(f1, c0)
    g = mm(f1, c1)
    h = mm(f2, c2)
    q = mm(b, c2)

    for i in range(16):
        pltpu.make_async_copy(ring.at[i], fbuf.at[i], f_r.at[i]).wait()
    for j in range(2):
        s8 = slice(8 * j, 8 * j + 8)
        m2 = keep_of(lines2, 2 * c + j)
        m3 = keep_of(lines3, 2 * c + j)
        fbuf[s8, :, W:2 * W] = (fbuf[s8, :, W:2 * W].astype(F32) * m2).astype(BF16)
        fbuf[s8, :, 2 * W:3 * W] = (fbuf[s8, :, 2 * W:3 * W].astype(F32) * m3).astype(BF16)

    def part(side, cols):
        f = fbuf[:, :, cols].reshape(512, HALF)
        out = jnp.dot(ahi[:, side].reshape(512, 512), f, preferred_element_type=F32)
        out = out + jnp.dot(alo[:, side].reshape(512, 512), f, preferred_element_type=F32)
        return out.reshape(4, 4, ROWS, HALF)

    alpha, beta = slice(0, HALF), slice(HALF, 2 * HALF)
    pair = []
    for i, cols in enumerate((alpha, beta)):
        ppar[:, :, :, cols] = part(1 - e, cols)
        cp = pltpu.make_async_remote_copy(
            src_ref=ppar.at[:, :, :, cols], dst_ref=prec.at[:, :, :, cols],
            send_sem=pr_s.at[i], recv_sem=pr_r.at[i], device_id=(z, partner), device_id_type=MESH)
        cp.start()
        pair.append(cp)
    for cols in (alpha, beta):
        pown[:, :, :, cols] = part(e, cols)

    def exchange(src, rec, send, recv, d, to):
        cp = pltpu.make_async_remote_copy(
            src_ref=src, dst_ref=rec.at[d - 1], send_sem=send.at[d - 1], recv_sem=recv.at[d - 1],
            device_id=(z, to), device_id_type=MESH)
        cp.start()
        return cp

    pair[0].wait_recv()
    pown[:, :, :, alpha] += prec[:, :, :, alpha]
    xa = [exchange(pown.at[:, (x + d) % 4, :, alpha], xra, xa_s, xa_r, d, col_of(y, (x + d) % 4))
          for d in (2, 1, 3)]
    pair[1].wait_recv()
    pown[:, :, :, beta] += prec[:, :, :, beta]
    xb = [exchange(pown.at[(y + d) % 4, :, :, beta], xrb, xb_s, xb_r, d, col_of((y + d) % 4, x))
          for d in (2, 1, 3)]
    for cp in xa:
        cp.wait_recv()
    ra[...] = pown[:, x, :, alpha] + xra[0] + xra[1] + xra[2]
    ya = [exchange(ra.at[(y + d) % 4], yra, ya_s, ya_r, d, col_of((y + d) % 4, x)) for d in (2, 1, 3)]
    for cp in xb:
        cp.wait_recv()
    rb[...] = pown[y, :, :, beta] + xrb[0] + xrb[1] + xrb[2]
    yb = [exchange(rb.at[(x + d) % 4], yrb, yb_s, yb_r, d, col_of(y, (x + d) % 4)) for d in (2, 1, 3)]
    for cp in ya:
        cp.wait_recv()
    ysum[:, alpha] = ra[y] + yra[0] + yra[1] + yra[2]
    for cp in yb:
        cp.wait_recv()
    ysum[:, beta] = rb[x] + yrb[0] + yrb[1] + yrb[2]

    y1 = ysum[:, 0:W]
    a = mm(y1, c0)
    w = mm(y1, c1)
    y2 = (ysum[:, W:2 * W] - a) * keep2
    v = mm(y2, c2)
    u = mm(a, c2)
    y3 = (ysum[:, 2 * W:3 * W] - w - v) * keep3
    o1[...] = -y1
    o2[...] = -y2
    o3[...] = -y3

    def add(i, right, left):
        val = tmm(jnp.concatenate(right, axis=0), jnp.concatenate(left, axis=0))
        phi[i] += val.reshape(4, 4, 2, 8, W)

    add(0, [y1], [f1])
    add(3, [f2, -a], [y1, f1])
    add(1, [y2, -f2, a], [f2, a, b])
    add(4, [f3 - h, u - w], [y1, f1])
    add(5, [f3, -(w + v), g + h, -u], [y2, f2, a, b])
    add(2, [y3, h - f3, w - u, -f3, w + v, -(g + h), u], [f3, w, g, v, h, u, q])

    qc = pltpu.make_async_remote_copy(
        src_ref=phi.at[:, :, :, 1 - e], dst_ref=qrec,
        send_sem=q_s.at[0], recv_sem=q_r.at[0], device_id=(z, partner), device_id_type=MESH)
    qc.start()
    qc.wait_recv()
    qrec[...] += phi[:, :, :, e]
    s2a = [exchange(qrec.at[0:3, :, (x + d) % 4], x2a, x2a_s, x2a_r, d, col_of(y, (x + d) % 4))
           for d in (2, 1, 3)]
    s2b = [exchange(qrec.at[3:6, (y + d) % 4], x2b, x2b_s, x2b_r, d, col_of((y + d) % 4, x))
           for d in (2, 1, 3)]
    for cp in s2a:
        cp.wait_recv()
    r2a[...] = qrec[0:3, :, x] + x2a[0] + x2a[1] + x2a[2]
    t2a = [exchange(r2a.at[:, (y + d) % 4], y2a, y2a_s, y2a_r, d, col_of((y + d) % 4, x)) for d in (2, 1, 3)]
    for cp in s2b:
        cp.wait_recv()
    r2b[...] = qrec[3:6, y] + x2b[0] + x2b[1] + x2b[2]
    t2b = [exchange(r2b.at[:, (x + d) % 4], y2b, y2b_s, y2b_r, d, col_of(y, (x + d) % 4)) for d in (2, 1, 3)]
    for cp in t2a:
        cp.wait_recv()
    sa = r2a[:, y] + y2a[0] + y2a[1] + y2a[2]
    for cp in t2b:
        cp.wait_recv()
    sb = r2b[:, x] + y2b[0] + y2b[1] + y2b[2]

    for zz in range(16):
        for i in range(6):
            src = sa[i] if i < 3 else sb[i - 3]
            zsend[zz, :, 16 * i:16 * i + 16] = src[:, 16 * zz:16 * zz + 16]
        zsend[zz, :, 96:128] = jnp.zeros((8, 32), F32)
    zc = []
    for d in (8, 7, 9, 6, 10, 5, 11, 4, 12, 3, 13, 2, 14, 1, 15):
        to = (z + d) % 16
        cp = pltpu.make_async_remote_copy(
            src_ref=zsend.at[to], dst_ref=zrec.at[d - 1], send_sem=z_s.at[d - 1], recv_sem=z_r.at[d - 1],
            device_id=(to, c), device_id_type=MESH)
        cp.start()
        zc.append(cp)
    for cp in zc:
        cp.wait_recv()
    tile = zsend[z]
    for d in range(15):
        tile = tile + zrec[d]
    turned = tile.T
    for i in range(6):
        ot[i] = turned[16 * i:16 * i + 16, :]

    for s in range(8):
        ring_copy(z, s, up_s, up_r, up).wait_send()
    for s in range(7):
        ring_copy(z, s, dn_s, dn_r, down).wait_send()
    for i in range(16):
        @pl.when((i * 2 + half) != c)
        def _():
            plane_copy(i).wait_send()
    for cp in pair + xa + xb + ya + yb + [qc] + s2a + s2b + t2a + t2b + zc:
        cp.wait_send()


def body(ancestor_inverse, panel_one, panel_two, panel_three, couplings, diag_terms, list_two, list_three):
    any_spec = pl.BlockSpec(memory_space=pl.ANY)
    vm = pl.BlockSpec(memory_space=pltpu.VMEM)
    dma = pltpu.SemaphoreType.DMA
    return pl.pallas_call(
        kernel,
        out_shape=(
            jax.ShapeDtypeStruct((ROWS, W), F32),
            jax.ShapeDtypeStruct((ROWS, W), F32),
            jax.ShapeDtypeStruct((ROWS, W), F32),
            jax.ShapeDtypeStruct((6, 16, 8), F32),
        ),
        in_specs=[any_spec] * 4 + [vm] * 4,
        out_specs=(vm,) * 4,
        scratch_shapes=[
            pltpu.VMEM((1024, 512), F32),
            pltpu.VMEM((16, 2, 32, 512), BF16),
            pltpu.VMEM((16, 2, 32, 512), BF16),
            pltpu.VMEM((16, ROWS, 768), BF16),
            pltpu.VMEM((16, ROWS, 768), BF16),
            pltpu.VMEM((4, 4, ROWS, 768), F32),
            pltpu.VMEM((4, 4, ROWS, 768), F32),
            pltpu.VMEM((4, 4, ROWS, 768), F32),
            pltpu.VMEM((3, 4, ROWS, HALF), F32),
            pltpu.VMEM((3, ROWS, HALF), F32),
            pltpu.VMEM((3, 4, ROWS, HALF), F32),
            pltpu.VMEM((3, ROWS, HALF), F32),
            pltpu.VMEM((4, ROWS, HALF), F32),
            pltpu.VMEM((4, ROWS, HALF), F32),
            pltpu.VMEM((ROWS, 768), F32),
            pltpu.VMEM((6, 4, 4, 2, 8, W), F32),
            pltpu.VMEM((6, 4, 4, 8, W), F32),
            pltpu.VMEM((3, 3, 4, 8, W), F32),
            pltpu.VMEM((3, 3, 8, W), F32),
            pltpu.VMEM((3, 3, 4, 8, W), F32),
            pltpu.VMEM((3, 3, 8, W), F32),
            pltpu.VMEM((3, 4, 8, W), F32),
            pltpu.VMEM((3, 4, 8, W), F32),
            pltpu.VMEM((16, 8, 128), F32),
            pltpu.VMEM((15, 8, 128), F32),
            dma((4,)), dma((8,)), dma((8,)), dma((7,)), dma((7,)), dma((16,)), dma((16,)), dma((2,)), dma((2,)),
            dma((3,)), dma((3,)), dma((3,)), dma((3,)), dma((3,)), dma((3,)), dma((3,)), dma((3,)),
            dma((1,)), dma((1,)), dma((3,)), dma((3,)), dma((3,)), dma((3,)), dma((3,)), dma((3,)),
            dma((3,)), dma((3,)), dma((15,)), dma((15,)),
        ],
        compiler_params=pltpu.CompilerParams(
            collective_id=0, has_side_effects=True, vmem_limit_bytes=56 << 20
        ),
        name="chain_inverse",
    )(
        ancestor_inverse, panel_one, panel_two, panel_three, couplings, diag_terms,
        list_two.reshape(1, -1), list_three.reshape(1, -1),
    )


def solution(mesh):
    rows = P(("row", "col"), None)
    return jax.shard_map(
        body,
        mesh=mesh,
        in_specs=(P("row", "col"), rows, rows, rows, P(), P(), P(), P()),
        out_specs=(rows, rows, rows, P(None, "row", "col")),
        check_vma=False,
    )
```

```python
import functools

import jax
import jax.numpy as jnp
from jax import lax
from jax.experimental import pallas as pl
from jax.experimental.pallas import tpu as pltpu
from jax.sharding import PartitionSpec as P

MESH = pl.DeviceIdType.MESH
HI = lax.Precision.HIGHEST
F32 = jnp.float32
BF16 = jnp.bfloat16
NZ, NK, W, ROWS = 16, 16, 256, 32
HALF = 384


def mm(a, b):
    return jnp.dot(a, b, precision=HI, preferred_element_type=F32)


def tmm(a, b):
    return lax.dot_general(a, b, (((0,), (0,)), ((), ())), precision=HI, preferred_element_type=F32)


def keep_of(lines, block):
    return jnp.max(jnp.where(lines == block, 1.0, 0.0).astype(F32))


def kernel(
    a_hbm, p1, p2, p3, coup, diag, l2, l3,
    o, ot,
    a_vm, ahi, alo, ring, fbuf, pown, ppar, prec,
    xra, yra, xrb, yrb, ra, rb, ysum,
    phi, qrec, x2a, y2a, x2b, y2b, r2a, r2b, zsend, zrec,
    lsem, up_s, up_r, dn_s, dn_r, f_s, f_r, pr_s, pr_r,
    xa_s, xa_r, ya_s, ya_r, xb_s, xb_r, yb_s, yb_r,
    q_s, q_r, x2a_s, x2a_r, y2a_s, y2a_r, x2b_s, x2b_r, y2b_s, y2b_r, z_s, z_r,
):
    z = lax.axis_index("row")
    c = lax.axis_index("col")
    e = c % 2
    k = c // 2
    y = k // 4
    x = k % 4
    half = y // 2
    partner = k * 2 + (1 - e)

    def col_of(yy, xx):
        return (yy * 4 + xx) * 2 + e

    acopy = pltpu.make_async_copy(a_hbm, a_vm, lsem.at[0])
    acopy.start()
    own = []
    for i, p in enumerate((p1, p2, p3)):
        cp = pltpu.make_async_copy(p, ring.at[z, :, pl.ds(i * W, W)], lsem.at[1 + i])
        cp.start()
        own.append(cp)

    barrier = pltpu.get_barrier_semaphore()
    for d in range(1, 32):
        pl.semaphore_signal(barrier, inc=1, device_id=(z, (c + d) % 32), device_id_type=MESH)
    for d in (1, 15):
        pl.semaphore_signal(barrier, inc=1, device_id=((z + d) % 16, c), device_id_type=MESH)

    for cp in own:
        cp.wait()
    pl.semaphore_wait(barrier, 33)

    up, down = (z + 1) % 16, (z + 15) % 16
    slot = (k % 8) * 2 + e

    def ring_copy(item, s, q, send, recv, to):
        part = ring.at[item, :, pl.ds(q * W, W)]
        return pltpu.make_async_remote_copy(
            src_ref=part, dst_ref=part, send_sem=send.at[3 * s + q], recv_sem=recv.at[3 * s + q],
            device_id=(to, c), device_id_type=MESH)

    def plane_copy(item):
        return pltpu.make_async_remote_copy(
            src_ref=ring.at[item], dst_ref=fbuf.at[slot], send_sem=f_s.at[item], recv_sem=f_r.at[slot],
            device_id=(z, item * 2 + half), device_id_type=MESH)

    def spread(item):
        mine = (item * 2 + half) == c

        @pl.when(mine)
        def _():
            pltpu.make_async_copy(ring.at[item], fbuf.at[slot], f_r.at[slot]).start()

        @pl.when(jnp.logical_not(mine))
        def _():
            plane_copy(item).start()

    for q in range(3):
        ring_copy(z, 0, q, up_s, up_r, up).start()
        ring_copy(z, 0, q, dn_s, dn_r, down).start()
    spread(z)
    for s in range(1, 9):
        below, above = (z + 16 - s) % 16, (z + s) % 16
        for q in range(3):
            ring_copy(below, s - 1, q, up_s, up_r, up).wait_recv()
            if s < 8:
                ring_copy(below, s, q, up_s, up_r, up).start()
                ring_copy(above, s - 1, q, dn_s, dn_r, down).wait_recv()
            if s < 7:
                ring_copy(above, s, q, dn_s, dn_r, down).start()
        spread(below)
        if s < 8:
            spread(above)

    lines2 = l2[...]
    lines3 = l3[...]
    block = (z * 32 + c) // 8
    keep2 = keep_of(lines2, block)
    keep3 = keep_of(lines3, block)
    c0 = coup[0].astype(F32)
    c1 = coup[1].astype(F32)
    c2 = coup[2].astype(F32)
    first = jnp.where((z == 0) & (c == 0), 1.0, 0.0).astype(F32)
    g1 = diag[0]
    h21 = -mm(g1, c0)
    g2 = diag[1] - tmm(c0, h21)
    h31 = -(mm(g1, c1) + mm(h21, c2))
    h32 = -(tmm(h21, c1) + mm(g2, c2))
    g3 = diag[2] - tmm(c1, h31) - tmm(c2, h32)
    for i, v in enumerate((g1, g2, g3, h21, h31, h32)):
        phi[i] = (v.T * first).reshape(4, 4, 2, 8, W)

    acopy.wait()

    @pl.loop(0, 16)
    def _(i):
        v = a_vm[pl.ds(pl.multiple_of(i * 64, 64), 64), :]
        hi = v.astype(BF16)
        ahi[i] = hi.reshape(2, 32, 512)
        alo[i] = (v - hi.astype(F32)).astype(BF16).reshape(2, 32, 512)

    for i in range(16):
        pltpu.make_async_copy(ring.at[i], fbuf.at[i], f_r.at[i]).wait()
    for j in range(2):
        s8 = slice(8 * j, 8 * j + 8)
        m2 = keep_of(lines2, 2 * c + j)
        m3 = keep_of(lines3, 2 * c + j)
        fbuf[s8, :, W:2 * W] = (fbuf[s8, :, W:2 * W].astype(F32) * m2).astype(BF16)
        fbuf[s8, :, 2 * W:3 * W] = (fbuf[s8, :, 2 * W:3 * W].astype(F32) * m3).astype(BF16)

    def part(side, cols):
        f = fbuf[:, :, cols].reshape(512, HALF)
        out = jnp.dot(ahi[:, side].reshape(512, 512), f, preferred_element_type=F32)
        out = out + jnp.dot(alo[:, side].reshape(512, 512), f, preferred_element_type=F32)
        return out.reshape(4, 4, ROWS, HALF)

    alpha, beta = slice(0, HALF), slice(HALF, 2 * HALF)
    pair = []
    for i, cols in enumerate((alpha, beta)):
        ppar[:, :, :, cols] = part(1 - e, cols)
        cp = pltpu.make_async_remote_copy(
            src_ref=ppar.at[:, :, :, cols], dst_ref=prec.at[:, :, :, cols],
            send_sem=pr_s.at[i], recv_sem=pr_r.at[i], device_id=(z, partner), device_id_type=MESH)
        cp.start()
        pair.append(cp)
    for cols in (alpha, beta):
        pown[:, :, :, cols] = part(e, cols)

    def exchange(src, rec, send, recv, d, to):
        cp = pltpu.make_async_remote_copy(
            src_ref=src, dst_ref=rec.at[d - 1], send_sem=send.at[d - 1], recv_sem=recv.at[d - 1],
            device_id=(z, to), device_id_type=MESH)
        cp.start()
        return cp

    def relay(view, rec, send, recv, p, right, left):
        def go(ref, n, to):
            cp = pltpu.make_async_remote_copy(
                src_ref=ref, dst_ref=rec.at[n], send_sem=send.at[n], recv_sem=recv.at[n],
                device_id=(z, to), device_id_type=MESH)
            cp.start()
            return cp

        far, after, before = (p + 2) % 4, (p + 1) % 4, (p + 3) % 4
        cps = [go(view(far, 0), 0, right), go(view(far, 1), 1, left),
               go(view(after, 1), 2, right), go(view(before, 0), 3, left)]

        def middle():
            for n, q, h, to in ((0, after, 0, right), (1, before, 1, left)):
                cps[n].wait_recv()
                ref = view(q, h)
                ref[...] += rec[n]
                cps.append(go(ref, 4 + n, to))

        def finish():
            for cp in cps[2:]:
                cp.wait_recv()
            return view(p, 0)[...] + rec[3] + rec[4], view(p, 1)[...] + rec[2] + rec[5]

        return cps, middle, finish

    xn, yn = [col_of(y, (x + d) % 4) for d in (1, 3)], [col_of((y + d) % 4, x) for d in (1, 3)]
    pair[0].wait_recv()
    pown[:, :, :, alpha] += prec[:, :, :, alpha]
    xa, xa_mid, xa_end = relay(lambda q, h: pown.at[2 * h:2 * h + 2, q, :, alpha], xra, xa_s, xa_r, x, *xn)
    pair[1].wait_recv()
    pown[:, :, :, beta] += prec[:, :, :, beta]
    xb, xb_mid, xb_end = relay(lambda q, h: pown.at[q, 2 * h:2 * h + 2, :, beta], xrb, xb_s, xb_r, y, *yn)
    xa_mid()
    xb_mid()

    f1 = ring[z, :, 0:W].astype(F32)
    f2 = ring[z, :, W:2 * W].astype(F32) * keep2
    f3 = ring[z, :, 2 * W:3 * W].astype(F32) * keep3
    b = mm(f1, c0)
    g = mm(f1, c1)
    h = mm(f2, c2)
    q = mm(b, c2)

    ra[0:2], ra[2:4] = xa_end()
    ya = [exchange(ra.at[(y + d) % 4], yra, ya_s, ya_r, d, col_of((y + d) % 4, x)) for d in (2, 1, 3)]
    rb[0:2], rb[2:4] = xb_end()
    yb = [exchange(rb.at[(x + d) % 4], yrb, yb_s, yb_r, d, col_of(y, (x + d) % 4)) for d in (2, 1, 3)]
    for cp in ya:
        cp.wait_recv()
    ysum[:, alpha] = ra[y] + yra[0] + yra[1] + yra[2]
    for cp in yb:
        cp.wait_recv()
    ysum[:, beta] = rb[x] + yrb[0] + yrb[1] + yrb[2]

    y1 = ysum[:, 0:W]
    a = mm(y1, c0)
    w = mm(y1, c1)
    y2 = (ysum[:, W:2 * W] - a) * keep2
    v = mm(y2, c2)
    u = mm(a, c2)
    y3 = (ysum[:, 2 * W:3 * W] - w - v) * keep3
    o[0] = -y1
    o[1] = -y2
    o[2] = -y3

    def add(i, right, left):
        val = tmm(jnp.concatenate(right, axis=0), jnp.concatenate(left, axis=0))
        phi[i] += val.reshape(4, 4, 2, 8, W)

    add(0, [y1], [f1])
    add(3, [f2, -a], [y1, f1])
    add(1, [y2, -f2, a], [f2, a, b])
    add(4, [f3 - h, u - w], [y1, f1])
    add(5, [f3, -(w + v), g + h, -u], [y2, f2, a, b])
    add(2, [y3, h - f3, w - u, -f3, w + v, -(g + h), u], [f3, w, g, v, h, u, q])

    qc = pltpu.make_async_remote_copy(
        src_ref=phi.at[:, :, :, 1 - e], dst_ref=qrec,
        send_sem=q_s.at[0], recv_sem=q_r.at[0], device_id=(z, partner), device_id_type=MESH)
    qc.start()
    qc.wait_recv()
    qrec[...] += phi[:, :, :, e]
    s2a, s2a_mid, s2a_end = relay(
        lambda q, h: qrec.at[0:3, 2 * h:2 * h + 2, q], x2a, x2a_s, x2a_r, x, *xn)
    s2b, s2b_mid, s2b_end = relay(
        lambda q, h: qrec.at[3:6, q, 2 * h:2 * h + 2], x2b, x2b_s, x2b_r, y, *yn)
    s2a_mid()
    s2b_mid()
    r2a[:, 0:2], r2a[:, 2:4] = s2a_end()
    t2a = [exchange(r2a.at[:, (y + d) % 4], y2a, y2a_s, y2a_r, d, col_of((y + d) % 4, x)) for d in (2, 1, 3)]
    r2b[:, 0:2], r2b[:, 2:4] = s2b_end()
    t2b = [exchange(r2b.at[:, (x + d) % 4], y2b, y2b_s, y2b_r, d, col_of(y, (x + d) % 4)) for d in (2, 1, 3)]
    for cp in t2a:
        cp.wait_recv()
    sa = r2a[:, y] + y2a[0] + y2a[1] + y2a[2]
    for cp in t2b:
        cp.wait_recv()
    sb = r2b[:, x] + y2b[0] + y2b[1] + y2b[2]

    for zz in range(16):
        for i in range(6):
            src = sa[i] if i < 3 else sb[i - 3]
            zsend[zz, :, 16 * i:16 * i + 16] = src[:, 16 * zz:16 * zz + 16]
        zsend[zz, :, 96:128] = jnp.zeros((8, 32), F32)
    zc = []
    for d in (8, 7, 9, 6, 10, 5, 11, 4, 12, 3, 13, 2, 14, 1, 15):
        to = (z + d) % 16
        cp = pltpu.make_async_remote_copy(
            src_ref=zsend.at[to], dst_ref=zrec.at[d - 1], send_sem=z_s.at[d - 1], recv_sem=z_r.at[d - 1],
            device_id=(to, c), device_id_type=MESH)
        cp.start()
        zc.append(cp)
    for cp in zc:
        cp.wait_recv()
    tile = zsend[z]
    for d in range(15):
        tile = tile + zrec[d]
    ot[...] = tile

    for q in range(3):
        for s in range(8):
            ring_copy(z, s, q, up_s, up_r, up).wait_send()
        for s in range(7):
            ring_copy(z, s, q, dn_s, dn_r, down).wait_send()
    for i in range(16):
        @pl.when((i * 2 + half) != c)
        def _():
            plane_copy(i).wait_send()
    for cp in pair + xa + xb + ya + yb + [qc] + s2a + s2b + t2a + t2b + zc:
        cp.wait_send()


def hand_out(blocks, tile, o1, o2, o3, ot):
    o1[...] = blocks[0]
    o2[...] = blocks[1]
    o3[...] = blocks[2]
    for i in range(6):
        ot[i] = tile[:, 16 * i:16 * i + 16]


def body(ancestor_inverse, panel_one, panel_two, panel_three, couplings, diag_terms, list_two, list_three):
    any_spec = pl.BlockSpec(memory_space=pl.ANY)
    vm = pl.BlockSpec(memory_space=pltpu.VMEM)
    dma = pltpu.SemaphoreType.DMA
    blocks, tile = pl.pallas_call(
        kernel,
        out_shape=(
            jax.ShapeDtypeStruct((3, ROWS, W), F32),
            jax.ShapeDtypeStruct((8, 128), F32),
        ),
        in_specs=[any_spec] * 4 + [vm] * 4,
        out_specs=(vm,) * 2,
        scratch_shapes=[
            pltpu.VMEM((1024, 512), F32),
            pltpu.VMEM((16, 2, 32, 512), BF16),
            pltpu.VMEM((16, 2, 32, 512), BF16),
            pltpu.VMEM((16, ROWS, 768), BF16),
            pltpu.VMEM((16, ROWS, 768), BF16),
            pltpu.VMEM((4, 4, ROWS, 768), F32),
            pltpu.VMEM((4, 4, ROWS, 768), F32),
            pltpu.VMEM((4, 4, ROWS, 768), F32),
            pltpu.VMEM((6, 2, ROWS, HALF), F32),
            pltpu.VMEM((3, ROWS, HALF), F32),
            pltpu.VMEM((6, 2, ROWS, HALF), F32),
            pltpu.VMEM((3, ROWS, HALF), F32),
            pltpu.VMEM((4, ROWS, HALF), F32),
            pltpu.VMEM((4, ROWS, HALF), F32),
            pltpu.VMEM((ROWS, 768), F32),
            pltpu.VMEM((6, 4, 4, 2, 8, W), F32),
            pltpu.VMEM((6, 4, 4, 8, W), F32),
            pltpu.VMEM((6, 3, 2, 8, W), F32),
            pltpu.VMEM((3, 3, 8, W), F32),
            pltpu.VMEM((6, 3, 2, 8, W), F32),
            pltpu.VMEM((3, 3, 8, W), F32),
            pltpu.VMEM((3, 4, 8, W), F32),
            pltpu.VMEM((3, 4, 8, W), F32),
            pltpu.VMEM((16, 8, 128), F32),
            pltpu.VMEM((15, 8, 128), F32),
            dma((4,)), dma((24,)), dma((24,)), dma((21,)), dma((21,)), dma((16,)), dma((16,)), dma((2,)), dma((2,)),
            dma((6,)), dma((6,)), dma((3,)), dma((3,)), dma((6,)), dma((6,)), dma((3,)), dma((3,)),
            dma((1,)), dma((1,)), dma((6,)), dma((6,)), dma((3,)), dma((3,)), dma((6,)), dma((6,)),
            dma((3,)), dma((3,)), dma((15,)), dma((15,)),
        ],
        compiler_params=pltpu.CompilerParams(
            collective_id=0, has_side_effects=True, vmem_limit_bytes=56 << 20
        ),
        name="chain_inverse",
    )(
        ancestor_inverse, panel_one, panel_two, panel_three, couplings, diag_terms,
        list_two.reshape(1, -1), list_three.reshape(1, -1),
    )
    *inverses, small = pl.pallas_call(
        hand_out,
        out_shape=(jax.ShapeDtypeStruct((ROWS, W), F32),) * 3 + (jax.ShapeDtypeStruct((6, 8, 16), F32),),
        in_specs=[vm] * 2,
        out_specs=(vm,) * 4,
        name="hand_out",
    )(blocks, tile)
    return (*inverses, jnp.swapaxes(small, 1, 2))


def solution(mesh):
    rows = P(("row", "col"), None)
    return jax.shard_map(
        body,
        mesh=mesh,
        in_specs=(P("row", "col"), rows, rows, rows, P(), P(), P(), P()),
        out_specs=(rows, rows, rows, P(None, "row", "col")),
        check_vma=False,
    )
```

```python
import functools

import jax
import jax.numpy as jnp
from jax import lax
from jax.experimental import pallas as pl
from jax.experimental.pallas import tpu as pltpu
from jax.sharding import PartitionSpec as P

MESH = pl.DeviceIdType.MESH
F32 = jnp.float32
BF16 = jnp.bfloat16
NZ, NK, W, ROWS = 16, 16, 256, 32
STREAMS = ((0, 256), (256, 512), (512, 640), (640, 768))


def halves(v):
    hi = v.astype(BF16)
    return hi, (v - hi.astype(F32)).astype(BF16)


def mm(v, c):
    hi, lo = halves(v)
    return jnp.dot(hi, c, preferred_element_type=F32) + jnp.dot(lo, c, preferred_element_type=F32)


def turned_dot(a, b):
    return lax.dot_general(a, b, (((0,), (0,)), ((), ())), preferred_element_type=F32)


def tmc(v, c):
    hi, lo = halves(v)
    return turned_dot(hi, c) + turned_dot(lo, c)


def ctm(c, v):
    hi, lo = halves(v)
    return turned_dot(c, hi) + turned_dot(c, lo)


def tmm(a, b):
    ah, al = halves(a)
    bh, bl = halves(b)
    return turned_dot(jnp.concatenate([ah, al, ah], axis=0), jnp.concatenate([bh, bh, bl], axis=0))


def keep_of(lines, block):
    return jnp.max(jnp.where(lines == block, 1.0, 0.0).astype(F32))


def kernel(
    a_hbm, p1, p2, p3, coup_hbm, diag_hbm, l2, l3,
    o, ot,
    a_vm, coup, diag, ahi, alo, ring, fbuf, pown, ppar, prec,
    rec0, rec1, rec2, rec3, far0, far1, far2, far3, mid0, mid1, mid2, mid3, ysum,
    phi, qrec, x2a, y2a, x2b, y2b, r2a, r2b, zsend, zrec,
    lsem, in_sem, up_s, up_r, dn_s, dn_r, f_s, f_r, pr_s, pr_r,
    rel_s, rel_r, far_s, far_r,
    q_s, q_r, x2a_s, x2a_r, y2a_s, y2a_r, x2b_s, x2b_r, y2b_s, y2b_r, z_s, z_r,
):
    z = lax.axis_index("row")
    c = lax.axis_index("col")
    e = c % 2
    k = c // 2
    y = k // 4
    x = k % 4
    half = y // 2
    partner = k * 2 + (1 - e)

    def col_of(yy, xx):
        return (yy * 4 + xx) * 2 + e

    own = []
    for i, p in enumerate((p1, p2, p3)):
        cp = pltpu.make_async_copy(p, ring.at[z, i], lsem.at[1 + i])
        cp.start()
        own.append(cp)
    acopy = pltpu.make_async_copy(a_hbm, a_vm, lsem.at[0])
    ccopy = pltpu.make_async_copy(coup_hbm, coup, lsem.at[4])
    dcopy = pltpu.make_async_copy(diag_hbm, diag, lsem.at[5])
    for cp in (acopy, ccopy, dcopy):
        cp.start()

    barrier = pltpu.get_barrier_semaphore()
    line = [partner]
    cross = []
    for d in (1, 2, 3):
        for ee in (0, 1):
            line.append((y * 4 + (x + d) % 4) * 2 + ee)
            cross.append(((y + d) % 4 * 4 + x) * 2 + ee)
    for to in line + cross:
        pl.semaphore_signal(barrier, inc=1, device_id=(z, to), device_id_type=MESH)
    for d in (1, 15):
        pl.semaphore_signal(barrier, inc=1, device_id=((z + d) % 16, c), device_id_type=MESH)
    for cp in own:
        cp.wait()
    pl.semaphore_wait(barrier, 15)
    for to in cross:
        pl.semaphore_signal(in_sem, inc=1, device_id=(z, to), device_id_type=MESH)

    up, down = (z + 1) % 16, (z + 15) % 16
    slot = (k % 8) * 2 + e

    def ring_copy(item, s, q, send, recv, to):
        part = ring.at[item, q]
        return pltpu.make_async_remote_copy(
            src_ref=part, dst_ref=part, send_sem=send.at[3 * s + q], recv_sem=recv.at[3 * s + q],
            device_id=(to, c), device_id_type=MESH)

    def plane_copy(item, q):
        return pltpu.make_async_remote_copy(
            src_ref=ring.at[item, q], dst_ref=fbuf.at[q, slot],
            send_sem=f_s.at[3 * item + q], recv_sem=f_r.at[3 * slot + q],
            device_id=(z, item * 2 + half), device_id_type=MESH)

    def spread(item, q):
        mine = (item * 2 + half) == c

        @pl.when(mine)
        def _():
            pltpu.make_async_copy(ring.at[item, q], fbuf.at[q, slot], f_r.at[3 * slot + q]).start()

        @pl.when(jnp.logical_not(mine))
        def _():
            plane_copy(item, q).start()

    for q in range(3):
        ring_copy(z, 0, q, up_s, up_r, up).start()
        ring_copy(z, 0, q, dn_s, dn_r, down).start()
    pl.semaphore_wait(in_sem, 6)
    for q in range(3):
        spread(z, q)
    for s in range(1, 9):
        below, above = (z + 16 - s) % 16, (z + s) % 16
        for q in range(3):
            ring_copy(below, s - 1, q, up_s, up_r, up).wait_recv()
            if s < 8:
                ring_copy(below, s, q, up_s, up_r, up).start()
                ring_copy(above, s - 1, q, dn_s, dn_r, down).wait_recv()
            if s < 7:
                ring_copy(above, s, q, dn_s, dn_r, down).start()
            spread(below, q)
            if s < 8:
                spread(above, q)

    lines2 = l2[...]
    lines3 = l3[...]
    block = (z * 32 + c) // 8
    keep2 = keep_of(lines2, block)
    keep3 = keep_of(lines3, block)
    acopy.wait()

    @pl.loop(0, 16)
    def _(i):
        hi, lo = halves(a_vm[pl.ds(pl.multiple_of(i * 64, 64), 64), :])
        ahi[i] = hi.reshape(2, 32, 512)
        alo[i] = lo.reshape(2, 32, 512)

    ccopy.wait()
    dcopy.wait()
    c0, c1, c2 = coup[0], coup[1], coup[2]
    f1 = ring[z, 0].astype(F32)
    f2 = ring[z, 1].astype(F32) * keep2
    f3 = ring[z, 2].astype(F32) * keep3
    b = mm(f1, c0)
    g = mm(f1, c1)
    h = mm(f2, c2)
    q_ = mm(b, c2)

    def arrived(q):
        for i in range(16):
            pltpu.make_async_copy(ring.at[i, q], fbuf.at[q, i], f_r.at[3 * i + q]).wait()
        if q:
            lines = lines2 if q == 1 else lines3
            for j in range(2):
                s8 = slice(8 * j, 8 * j + 8)
                fbuf[q, s8] = (fbuf[q, s8].astype(F32) * keep_of(lines, 2 * c + j)).astype(BF16)

    def part(side, q):
        f = fbuf[q].reshape(512, W)
        out = jnp.dot(ahi[:, side].reshape(512, 512), f, preferred_element_type=F32)
        out = out + jnp.dot(alo[:, side].reshape(512, 512), f, preferred_element_type=F32)
        return out.reshape(4, 4, ROWS, W)

    def panel(q):
        return pl.ds(q * W, W)

    pair = []

    def to_partner(q):
        ppar[:, :, :, panel(q)] = part(1 - e, q)
        cp = pltpu.make_async_remote_copy(
            src_ref=ppar.at[:, :, :, panel(q)], dst_ref=prec.at[:, :, :, panel(q)],
            send_sem=pr_s.at[q], recv_sem=pr_r.at[q], device_id=(z, partner), device_id_type=MESH)
        cp.start()
        pair.append(cp)

    def from_partner(q):
        pair[q].wait_recv()
        pown[:, :, :, panel(q)] += prec[:, :, :, panel(q)]

    def exchange(src, rec, send, recv, d, to, n=0):
        cp = pltpu.make_async_remote_copy(
            src_ref=src, dst_ref=rec.at[d - 1], send_sem=send.at[n + d - 1], recv_sem=recv.at[n + d - 1],
            device_id=(z, to), device_id_type=MESH)
        cp.start()
        return cp

    def relay(view, rec, send, recv, p, right, left, base=0):
        def go(ref, n, to):
            cp = pltpu.make_async_remote_copy(
                src_ref=ref, dst_ref=rec.at[n], send_sem=send.at[base + n], recv_sem=recv.at[base + n],
                device_id=(z, to), device_id_type=MESH)
            cp.start()
            return cp

        far, after, before = (p + 2) % 4, (p + 1) % 4, (p + 3) % 4
        cps = [go(view(far, 0), 0, right), go(view(far, 1), 1, left),
               go(view(after, 1), 2, right), go(view(before, 0), 3, left)]

        def middle():
            for n, q, h, to in ((0, after, 0, right), (1, before, 1, left)):
                cps[n].wait_recv()
                ref = view(q, h)
                ref[...] += rec[n]
                cps.append(go(ref, 4 + n, to))

        def finish():
            for cp in cps[2:]:
                cp.wait_recv()
            return view(p, 0)[...] + rec[3] + rec[4], view(p, 1)[...] + rec[2] + rec[5]

        return cps, middle, finish

    xn, yn = [col_of(y, (x + d) % 4) for d in (1, 3)], [col_of((y + d) % 4, x) for d in (1, 3)]
    recs, mids, fars = (rec0, rec1, rec2, rec3), (mid0, mid1, mid2, mid3), (far0, far1, far2, far3)
    mid_of, end_of, second = [], [], [[], [], [], []]

    def open_stream(n):
        lo, hi = STREAMS[n]
        if n % 2 == 0:
            r = relay(lambda q, h: pown.at[2 * h:2 * h + 2, q, :, lo:hi], recs[n], rel_s, rel_r, x, *xn, base=6 * n)
        else:
            r = relay(lambda q, h: pown.at[q, 2 * h:2 * h + 2, :, lo:hi], recs[n], rel_s, rel_r, y, *yn, base=6 * n)
        mid_of.append((r[1], r[0]))
        end_of.append(r[2])

    def second_stage(n):
        mids[n][0:2], mids[n][2:4] = end_of[n]()
        for d in (2, 1, 3):
            if n % 2 == 0:
                src, to = mids[n].at[(y + d) % 4], col_of((y + d) % 4, x)
            else:
                src, to = mids[n].at[(x + d) % 4], col_of(y, (x + d) % 4)
            second[n].append(exchange(src, fars[n], far_s, far_r, d, to, n=3 * n))

    def close_stream(n):
        for cp in second[n]:
            cp.wait_recv()
        lo, hi = STREAMS[n]
        own_part = mids[n][y if n % 2 == 0 else x]
        ysum[:, lo:hi] = own_part + fars[n][0] + fars[n][1] + fars[n][2]

    arrived(0)
    to_partner(0)
    pown[:, :, :, panel(0)] = part(e, 0)
    arrived(1)
    to_partner(1)
    from_partner(0)
    open_stream(0)
    pown[:, :, :, panel(1)] = part(e, 1)
    arrived(2)
    to_partner(2)
    from_partner(1)
    open_stream(1)
    pown[:, :, :, panel(2)] = part(e, 2)
    mid_of[0][0]()
    from_partner(2)
    open_stream(2)
    open_stream(3)
    mid_of[1][0]()
    second_stage(0)
    mid_of[2][0]()
    mid_of[3][0]()

    first = jnp.where((z == 0) & (c == 0), 1.0, 0.0).astype(F32)
    g1 = diag[0]
    h21 = -mm(g1, c0)
    g2 = diag[1] - ctm(c0, h21)
    h31 = -(mm(g1, c1) + mm(h21, c2))
    h32 = -(tmc(h21, c1) + mm(g2, c2))
    g3 = diag[2] - ctm(c1, h31) - ctm(c2, h32)
    for i, v in enumerate((g1, g2, g3, h21, h31, h32)):
        phi[i] = (v.T * first).reshape(4, 4, 2, 8, W)

    second_stage(1)
    second_stage(2)
    second_stage(3)
    for n in range(4):
        close_stream(n)

    y1 = ysum[:, 0:W]
    a = mm(y1, c0)
    w = mm(y1, c1)
    y2 = (ysum[:, W:2 * W] - a) * keep2
    v = mm(y2, c2)
    u = mm(a, c2)
    y3 = (ysum[:, 2 * W:3 * W] - w - v) * keep3
    o[0] = -y1
    o[1] = -y2
    o[2] = -y3

    def add(i, right, left):
        val = tmm(jnp.concatenate(right, axis=0), jnp.concatenate(left, axis=0))
        phi[i] += val.reshape(4, 4, 2, 8, W)

    add(0, [y1], [f1])
    add(3, [f2, -a], [y1, f1])
    add(1, [y2, -f2, a], [f2, a, b])
    add(4, [f3 - h, u - w], [y1, f1])
    add(5, [f3, -(w + v), g + h, -u], [y2, f2, a, b])
    add(2, [y3, h - f3, w - u, -f3, w + v, -(g + h), u], [f3, w, g, v, h, u, q_])

    qc = pltpu.make_async_remote_copy(
        src_ref=phi.at[:, :, :, 1 - e], dst_ref=qrec,
        send_sem=q_s.at[0], recv_sem=q_r.at[0], device_id=(z, partner), device_id_type=MESH)
    qc.start()
    qc.wait_recv()
    qrec[...] += phi[:, :, :, e]
    s2a, s2a_mid, s2a_end = relay(
        lambda q, h: qrec.at[0:3, 2 * h:2 * h + 2, q], x2a, x2a_s, x2a_r, x, *xn)
    s2b, s2b_mid, s2b_end = relay(
        lambda q, h: qrec.at[3:6, q, 2 * h:2 * h + 2], x2b, x2b_s, x2b_r, y, *yn)
    s2a_mid()
    s2b_mid()
    r2a[:, 0:2], r2a[:, 2:4] = s2a_end()
    t2a = [exchange(r2a.at[:, (y + d) % 4], y2a, y2a_s, y2a_r, d, col_of((y + d) % 4, x)) for d in (2, 1, 3)]
    r2b[:, 0:2], r2b[:, 2:4] = s2b_end()
    t2b = [exchange(r2b.at[:, (x + d) % 4], y2b, y2b_s, y2b_r, d, col_of(y, (x + d) % 4)) for d in (2, 1, 3)]
    for cp in t2a:
        cp.wait_recv()
    sa = r2a[:, y] + y2a[0] + y2a[1] + y2a[2]
    for cp in t2b:
        cp.wait_recv()
    sb = r2b[:, x] + y2b[0] + y2b[1] + y2b[2]

    for zz in range(16):
        for i in range(6):
            src = sa[i] if i < 3 else sb[i - 3]
            zsend[zz, :, 16 * i:16 * i + 16] = src[:, 16 * zz:16 * zz + 16]
        zsend[zz, :, 96:128] = jnp.zeros((8, 32), F32)
    zc = []
    for d in (8, 7, 9, 6, 10, 5, 11, 4, 12, 3, 13, 2, 14, 1, 15):
        to = (z + d) % 16
        cp = pltpu.make_async_remote_copy(
            src_ref=zsend.at[to], dst_ref=zrec.at[d - 1], send_sem=z_s.at[d - 1], recv_sem=z_r.at[d - 1],
            device_id=(to, c), device_id_type=MESH)
        cp.start()
        zc.append(cp)
    for cp in zc:
        cp.wait_recv()
    tile = zsend[z]
    for d in range(15):
        tile = tile + zrec[d]
    ot[...] = tile

    for q in range(3):
        for s in range(8):
            ring_copy(z, s, q, up_s, up_r, up).wait_send()
        for s in range(7):
            ring_copy(z, s, q, dn_s, dn_r, down).wait_send()
    for i in range(16):
        @pl.when((i * 2 + half) != c)
        def _():
            for q in range(3):
                plane_copy(i, q).wait_send()
    near = [cp for _, cps in mid_of for cp in cps]
    for cp in pair + near + second[0] + second[1] + second[2] + second[3] + [qc] + s2a + s2b + t2a + t2b + zc:
        cp.wait_send()


def hand_out(blocks, tile, o1, o2, o3, ot):
    o1[...] = blocks[0]
    o2[...] = blocks[1]
    o3[...] = blocks[2]
    for i in range(6):
        ot[i] = tile[:, 16 * i:16 * i + 16]


def body(ancestor_inverse, panel_one, panel_two, panel_three, couplings, diag_terms, list_two, list_three):
    any_spec = pl.BlockSpec(memory_space=pl.ANY)
    vm = pl.BlockSpec(memory_space=pltpu.VMEM)
    dma = pltpu.SemaphoreType.DMA
    blocks, tile = pl.pallas_call(
        kernel,
        out_shape=(
            jax.ShapeDtypeStruct((3, ROWS, W), F32),
            jax.ShapeDtypeStruct((8, 128), F32),
        ),
        in_specs=[any_spec] * 6 + [vm] * 2,
        out_specs=(vm,) * 2,
        scratch_shapes=[
            pltpu.VMEM((1024, 512), F32),
            pltpu.VMEM((3, W, W), BF16),
            pltpu.VMEM((3, W, W), F32),
            pltpu.VMEM((16, 2, 32, 512), BF16),
            pltpu.VMEM((16, 2, 32, 512), BF16),
            pltpu.VMEM((16, 3, ROWS, W), BF16),
            pltpu.VMEM((3, 16, ROWS, W), BF16),
            pltpu.VMEM((4, 4, ROWS, 768), F32),
            pltpu.VMEM((4, 4, ROWS, 768), F32),
            pltpu.VMEM((4, 4, ROWS, 768), F32),
            *[pltpu.VMEM((6, 2, ROWS, hi - lo), F32) for lo, hi in STREAMS],
            *[pltpu.VMEM((3, ROWS, hi - lo), F32) for lo, hi in STREAMS],
            *[pltpu.VMEM((4, ROWS, hi - lo), F32) for lo, hi in STREAMS],
            pltpu.VMEM((ROWS, 768), F32),
            pltpu.VMEM((6, 4, 4, 2, 8, W), F32),
            pltpu.VMEM((6, 4, 4, 8, W), F32),
            pltpu.VMEM((6, 3, 2, 8, W), F32),
            pltpu.VMEM((3, 3, 8, W), F32),
            pltpu.VMEM((6, 3, 2, 8, W), F32),
            pltpu.VMEM((3, 3, 8, W), F32),
            pltpu.VMEM((3, 4, 8, W), F32),
            pltpu.VMEM((3, 4, 8, W), F32),
            pltpu.VMEM((16, 8, 128), F32),
            pltpu.VMEM((15, 8, 128), F32),
            dma((6,)), pltpu.SemaphoreType.REGULAR,
            dma((24,)), dma((24,)), dma((21,)), dma((21,)), dma((48,)), dma((48,)), dma((3,)), dma((3,)),
            dma((24,)), dma((24,)), dma((12,)), dma((12,)),
            dma((1,)), dma((1,)), dma((6,)), dma((6,)), dma((3,)), dma((3,)), dma((6,)), dma((6,)),
            dma((3,)), dma((3,)), dma((15,)), dma((15,)),
        ],
        compiler_params=pltpu.CompilerParams(
            collective_id=0, has_side_effects=True, vmem_limit_bytes=56 << 20
        ),
        name="chain_inverse",
    )(
        ancestor_inverse, panel_one, panel_two, panel_three, couplings, diag_terms,
        list_two.reshape(1, -1), list_three.reshape(1, -1),
    )
    *inverses, small = pl.pallas_call(
        hand_out,
        out_shape=(jax.ShapeDtypeStruct((ROWS, W), F32),) * 3 + (jax.ShapeDtypeStruct((6, 8, 16), F32),),
        in_specs=[vm] * 2,
        out_specs=(vm,) * 4,
        name="hand_out",
    )(blocks, tile)
    return (*inverses, jnp.swapaxes(small, 1, 2))


def solution(mesh):
    rows = P(("row", "col"), None)
    return jax.shard_map(
        body,
        mesh=mesh,
        in_specs=(P("row", "col"), rows, rows, rows, P(), P(), P(), P()),
        out_specs=(rows, rows, rows, P(None, "row", "col")),
        check_vma=False,
    )
```

```python
import functools

import jax
import jax.numpy as jnp
from jax import lax
from jax.experimental import pallas as pl
from jax.experimental.pallas import tpu as pltpu
from jax.sharding import PartitionSpec as P

MESH = pl.DeviceIdType.MESH
F32 = jnp.float32
BF16 = jnp.bfloat16
NZ, NK, W, ROWS = 16, 16, 256, 32
REACH = {1: 8, -1: 7}
GROUPS = ((0, 0, 256, True), (3, 0, 128, True), (3, 128, 256, False))
STREAMS = ((0, 256), (256, 512), (512, 640), (640, 768))


def halves(v):
    hi = v.astype(BF16)
    return hi, (v - hi.astype(F32)).astype(BF16)


def mm(v, c):
    hi, lo = halves(v)
    return jnp.dot(hi, c, preferred_element_type=F32) + jnp.dot(lo, c, preferred_element_type=F32)


def turned_dot(a, b):
    return lax.dot_general(a, b, (((0,), (0,)), ((), ())), preferred_element_type=F32)


def tmc(v, c):
    hi, lo = halves(v)
    return turned_dot(hi, c) + turned_dot(lo, c)


def ctm(c, v):
    hi, lo = halves(v)
    return turned_dot(c, hi) + turned_dot(c, lo)


def tmm(a, b):
    ah, al = halves(a)
    bh, bl = halves(b)
    return turned_dot(jnp.concatenate([ah, al, ah], axis=0), jnp.concatenate([bh, bh, bl], axis=0))


def keep_of(lines, block):
    return jnp.max(jnp.where(lines == block, 1.0, 0.0).astype(F32))


def kernel(
    a_hbm, p1, p2, p3, coup_hbm, diag_hbm, l2, l3,
    o, ot,
    a_vm, coup, diag, ahi, alo, ring, fbuf, pown, ppar, prec,
    rec0, rec1, rec2, rec3, far0, far1, far2, far3, mid0, mid1, mid2, mid3, ysum,
    phi, qrec, ga_rec, gb_rec, gc_rec, ga_far, gb_far, gc_far, ga_mid, gb_mid, gc_mid, zsend, zrec,
    lsem, in_sem, up_s, up_r, dn_s, dn_r, f_s, f_r, pr_s, pr_r,
    rel_s, rel_r, far_s, far_r,
    q_s, q_r, g_s, g_r, gf_s, gf_r, z_s, z_r,
):
    z = lax.axis_index("row")
    c = lax.axis_index("col")
    e = c % 2
    k = c // 2
    y = k // 4
    x = k % 4
    half = y // 2
    partner = k * 2 + (1 - e)

    def col_of(yy, xx):
        return (yy * 4 + xx) * 2 + e

    own = []
    for i, p in enumerate((p1, p2, p3)):
        cp = pltpu.make_async_copy(p, ring.at[z, i], lsem.at[1 + i])
        cp.start()
        own.append(cp)
    acopy = pltpu.make_async_copy(a_hbm, a_vm, lsem.at[0])
    ccopy = pltpu.make_async_copy(coup_hbm, coup, lsem.at[4])
    dcopy = pltpu.make_async_copy(diag_hbm, diag, lsem.at[5])
    for cp in (acopy, ccopy, dcopy):
        cp.start()

    barrier = pltpu.get_barrier_semaphore()
    line = [partner]
    cross = []
    for d in (1, 2, 3):
        for ee in (0, 1):
            line.append((y * 4 + (x + d) % 4) * 2 + ee)
            cross.append(((y + d) % 4 * 4 + x) * 2 + ee)
    for to in line + cross:
        pl.semaphore_signal(barrier, inc=1, device_id=(z, to), device_id_type=MESH)
    for d in (1, 2, 14, 15):
        pl.semaphore_signal(barrier, inc=1, device_id=((z + d) % 16, c), device_id_type=MESH)
    for cp in own:
        cp.wait()
    pl.semaphore_wait(barrier, 17)
    for to in cross:
        pl.semaphore_signal(in_sem, inc=1, device_id=(z, to), device_id_type=MESH)

    slot = (k % 8) * 2 + e

    def hop(item, dist, step, q, way):
        send, recv = (up_s, up_r) if way > 0 else (dn_s, dn_r)
        part = ring.at[item, q]
        n = 3 * (dist + step - 1) + q
        return pltpu.make_async_remote_copy(
            src_ref=part, dst_ref=part, send_sem=send.at[n], recv_sem=recv.at[n],
            device_id=((z + 16 + way * step) % 16, c), device_id_type=MESH)

    def item_at(dist, way):
        return (z + 16 - way * dist) % 16

    def push(dist, q, way):
        for step in (2, 1):
            if dist + step <= REACH[way]:
                hop(item_at(dist, way), dist, step, q, way).start()

    def landed(dist, q, way):
        hop(item_at(dist, way), dist - 1, 1, q, way).wait_recv()

    def plane_copy(item, q):
        return pltpu.make_async_remote_copy(
            src_ref=ring.at[item, q], dst_ref=fbuf.at[q, slot],
            send_sem=f_s.at[3 * item + q], recv_sem=f_r.at[3 * slot + q],
            device_id=(z, item * 2 + half), device_id_type=MESH)

    def spread(item, q):
        mine = (item * 2 + half) == c

        @pl.when(mine)
        def _():
            pltpu.make_async_copy(ring.at[item, q], fbuf.at[q, slot], f_r.at[3 * slot + q]).start()

        @pl.when(jnp.logical_not(mine))
        def _():
            plane_copy(item, q).start()

    for q in range(3):
        for way in (1, -1):
            push(0, q, way)
    pl.semaphore_wait(in_sem, 6)
    for q in range(3):
        spread(z, q)
    for dist in (2, 4, 6, 8):
        for at in (dist, dist - 1):
            for q in range(3):
                for way in (1, -1):
                    if at <= REACH[way]:
                        landed(at, q, way)
                        if at == dist:
                            push(at, q, way)
                        spread(item_at(at, way), q)

    lines2 = l2[...]
    lines3 = l3[...]
    block = (z * 32 + c) // 8
    keep2 = keep_of(lines2, block)
    keep3 = keep_of(lines3, block)
    acopy.wait()

    @pl.loop(0, 16)
    def _(i):
        hi, lo = halves(a_vm[pl.ds(pl.multiple_of(i * 64, 64), 64), :])
        ahi[i] = hi.reshape(2, 32, 512)
        alo[i] = lo.reshape(2, 32, 512)

    ccopy.wait()
    dcopy.wait()
    c0, c1, c2 = coup[0], coup[1], coup[2]
    f1 = ring[z, 0].astype(F32)
    f2 = ring[z, 1].astype(F32) * keep2
    f3 = ring[z, 2].astype(F32) * keep3
    b = mm(f1, c0)
    g = mm(f1, c1)
    h = mm(f2, c2)
    q_ = mm(b, c2)

    def arrived(q):
        for i in range(16):
            pltpu.make_async_copy(ring.at[i, q], fbuf.at[q, i], f_r.at[3 * i + q]).wait()
        if q:
            lines = lines2 if q == 1 else lines3
            for j in range(2):
                s8 = slice(8 * j, 8 * j + 8)
                fbuf[q, s8] = (fbuf[q, s8].astype(F32) * keep_of(lines, 2 * c + j)).astype(BF16)

    def part(side, q):
        f = fbuf[q].reshape(512, W)
        out = jnp.dot(ahi[:, side].reshape(512, 512), f, preferred_element_type=F32)
        out = out + jnp.dot(alo[:, side].reshape(512, 512), f, preferred_element_type=F32)
        return out.reshape(4, 4, ROWS, W)

    def panel(q):
        return pl.ds(q * W, W)

    pair = []

    def to_partner(q):
        ppar[:, :, :, panel(q)] = part(1 - e, q)
        cp = pltpu.make_async_remote_copy(
            src_ref=ppar.at[:, :, :, panel(q)], dst_ref=prec.at[:, :, :, panel(q)],
            send_sem=pr_s.at[q], recv_sem=pr_r.at[q], device_id=(z, partner), device_id_type=MESH)
        cp.start()
        pair.append(cp)

    def from_partner(q):
        pair[q].wait_recv()
        pown[:, :, :, panel(q)] += prec[:, :, :, panel(q)]

    def exchange(src, rec, send, recv, d, to, n=0):
        cp = pltpu.make_async_remote_copy(
            src_ref=src, dst_ref=rec.at[d - 1], send_sem=send.at[n + d - 1], recv_sem=recv.at[n + d - 1],
            device_id=(z, to), device_id_type=MESH)
        cp.start()
        return cp

    def relay(view, rec, send, recv, p, right, left, base=0):
        def go(ref, n, to):
            cp = pltpu.make_async_remote_copy(
                src_ref=ref, dst_ref=rec.at[n], send_sem=send.at[base + n], recv_sem=recv.at[base + n],
                device_id=(z, to), device_id_type=MESH)
            cp.start()
            return cp

        far, after, before = (p + 2) % 4, (p + 1) % 4, (p + 3) % 4
        cps = [go(view(far, 0), 0, right), go(view(far, 1), 1, left),
               go(view(after, 1), 2, right), go(view(before, 0), 3, left)]

        def middle():
            for n, q, h, to in ((0, after, 0, right), (1, before, 1, left)):
                cps[n].wait_recv()
                ref = view(q, h)
                ref[...] += rec[n]
                cps.append(go(ref, 4 + n, to))

        def finish():
            for cp in cps[2:]:
                cp.wait_recv()
            return view(p, 0)[...] + rec[3] + rec[4], view(p, 1)[...] + rec[2] + rec[5]

        return cps, middle, finish

    xn, yn = [col_of(y, (x + d) % 4) for d in (1, 3)], [col_of((y + d) % 4, x) for d in (1, 3)]
    recs, mids, fars = (rec0, rec1, rec2, rec3), (mid0, mid1, mid2, mid3), (far0, far1, far2, far3)
    mid_of, end_of, second = [], [], [[], [], [], []]

    def open_stream(n):
        lo, hi = STREAMS[n]
        if n % 2 == 0:
            r = relay(lambda q, h: pown.at[2 * h:2 * h + 2, q, :, lo:hi], recs[n], rel_s, rel_r, x, *xn, base=6 * n)
        else:
            r = relay(lambda q, h: pown.at[q, 2 * h:2 * h + 2, :, lo:hi], recs[n], rel_s, rel_r, y, *yn, base=6 * n)
        mid_of.append((r[1], r[0]))
        end_of.append(r[2])

    def second_stage(n):
        mids[n][0:2], mids[n][2:4] = end_of[n]()
        for d in (2, 1, 3):
            if n % 2 == 0:
                src, to = mids[n].at[(y + d) % 4], col_of((y + d) % 4, x)
            else:
                src, to = mids[n].at[(x + d) % 4], col_of(y, (x + d) % 4)
            second[n].append(exchange(src, fars[n], far_s, far_r, d, to, n=3 * n))

    def close_stream(n):
        for cp in second[n]:
            cp.wait_recv()
        lo, hi = STREAMS[n]
        own_part = mids[n][y if n % 2 == 0 else x]
        ysum[:, lo:hi] = own_part + fars[n][0] + fars[n][1] + fars[n][2]

    arrived(0)
    to_partner(0)
    pown[:, :, :, panel(0)] = part(e, 0)
    arrived(1)
    to_partner(1)
    from_partner(0)
    open_stream(0)
    pown[:, :, :, panel(1)] = part(e, 1)
    arrived(2)
    to_partner(2)
    from_partner(1)
    open_stream(1)
    pown[:, :, :, panel(2)] = part(e, 2)
    mid_of[0][0]()
    from_partner(2)
    open_stream(2)
    open_stream(3)
    mid_of[1][0]()
    second_stage(0)
    mid_of[2][0]()
    mid_of[3][0]()

    first = jnp.where((z == 0) & (c == 0), 1.0, 0.0).astype(F32)
    g1 = diag[0]
    h21 = -mm(g1, c0)
    g2 = diag[1] - ctm(c0, h21)
    h31 = -(mm(g1, c1) + mm(h21, c2))
    h32 = -(tmc(h21, c1) + mm(g2, c2))
    g3 = diag[2] - ctm(c1, h31) - ctm(c2, h32)
    for i, v in enumerate((g1, h21, h31, g2, h32, g3)):
        phi[i] = (v.T * first).reshape(4, 4, 2, 8, W)

    second_stage(1)
    second_stage(2)
    second_stage(3)
    def add(i, right, left):
        val = tmm(jnp.concatenate(right, axis=0), jnp.concatenate(left, axis=0))
        phi[i] += val.reshape(4, 4, 2, 8, W)

    def pair_terms(n):
        three = slice(3 * n, 3 * n + 3)
        cp = pltpu.make_async_remote_copy(
            src_ref=phi.at[three, :, :, 1 - e], dst_ref=qrec.at[three],
            send_sem=q_s.at[n], recv_sem=q_r.at[n], device_id=(z, partner), device_id_type=MESH)
        cp.start()
        return cp

    group_far = (ga_far, gb_far, gc_far)
    group_mid = (ga_mid, gb_mid, gc_mid)
    group_rec = (ga_rec, gb_rec, gc_rec)
    groups = {}

    def open_group(n):
        blk, lo, hi, xfirst = GROUPS[n]
        three = slice(blk, blk + 3)
        if xfirst:
            r = relay(lambda q, h: qrec.at[three, 2 * h:2 * h + 2, q, :, lo:hi],
                      group_rec[n], g_s, g_r, x, *xn, base=6 * n)
        else:
            r = relay(lambda q, h: qrec.at[three, q, 2 * h:2 * h + 2, :, lo:hi],
                      group_rec[n], g_s, g_r, y, *yn, base=6 * n)
        groups[n] = r

    def second_group(n):
        xfirst = GROUPS[n][3]
        group_mid[n][:, 0:2], group_mid[n][:, 2:4] = groups[n][2]()
        cps = []
        for d in (2, 1, 3):
            if xfirst:
                src, to = group_mid[n].at[:, (y + d) % 4], col_of((y + d) % 4, x)
            else:
                src, to = group_mid[n].at[:, (x + d) % 4], col_of(y, (x + d) % 4)
            cps.append(exchange(src, group_far[n], gf_s, gf_r, d, to, n=3 * n))
        return cps

    def close_group(n, cps):
        for cp in cps:
            cp.wait_recv()
        far = group_far[n]
        return group_mid[n][:, y if GROUPS[n][3] else x] + far[0] + far[1] + far[2]

    def pack(blk, val):
        for zz in range(16):
            for i in range(3):
                at = 16 * (blk + i)
                zsend[zz, :, at:at + 16] = val[i][:, 16 * zz:16 * zz + 16]

    close_stream(0)
    y1 = ysum[:, 0:W]
    a = mm(y1, c0)
    w = mm(y1, c1)
    u = mm(a, c2)
    add(0, [y1], [f1])
    add(1, [f2, -a], [y1, f1])
    add(2, [f3 - h, u - w], [y1, f1])
    terms = [pair_terms(0)]
    o[0] = -y1
    close_stream(1)
    y2 = (ysum[:, W:2 * W] - a) * keep2
    o[1] = -y2
    v = mm(y2, c2)
    add(3, [y2, -f2, a], [f2, a, b])
    add(4, [f3, -(w + v), g + h, -u], [y2, f2, a, b])
    close_stream(2)
    close_stream(3)
    terms[0].wait_recv()
    qrec[0:3] += phi[0:3, :, :, e]
    open_group(0)
    y3 = (ysum[:, 2 * W:3 * W] - w - v) * keep3
    add(5, [y3, h - f3, w - u, -f3, w + v, -(g + h), u], [f3, w, g, v, h, u, q_])
    terms.append(pair_terms(1))
    o[2] = -y3
    groups[0][1]()
    terms[1].wait_recv()
    qrec[3:6] += phi[3:6, :, :, e]
    open_group(1)
    open_group(2)
    last = [second_group(0)]
    groups[1][1]()
    groups[2][1]()
    for zz in range(16):
        zsend[zz, :, 96:128] = jnp.zeros((8, 32), F32)
    pack(0, close_group(0, last[0]))
    last.append(second_group(1))
    last.append(second_group(2))
    left = close_group(1, last[1])
    right = close_group(2, last[2])
    pack(3, jnp.concatenate([left, right], axis=2))

    zc = []
    for d in (8, 7, 9, 6, 10, 5, 11, 4, 12, 3, 13, 2, 14, 1, 15):
        to = (z + d) % 16
        cp = pltpu.make_async_remote_copy(
            src_ref=zsend.at[to], dst_ref=zrec.at[d - 1], send_sem=z_s.at[d - 1], recv_sem=z_r.at[d - 1],
            device_id=(to, c), device_id_type=MESH)
        cp.start()
        zc.append(cp)
    for cp in zc:
        cp.wait_recv()
    tile = zsend[z]
    for d in range(15):
        tile = tile + zrec[d]
    ot[...] = tile

    for way in (1, -1):
        for dist in range(1, REACH[way] + 1):
            for q in range(3):
                hop(z, dist - 1, 1, q, way).wait_send()
    for i in range(16):
        @pl.when((i * 2 + half) != c)
        def _():
            for q in range(3):
                plane_copy(i, q).wait_send()
    near = [cp for _, cps in mid_of for cp in cps]
    near += [cp for n in range(3) for cp in groups[n][0] + last[n]]
    for cp in pair + near + second[0] + second[1] + second[2] + second[3] + terms + zc:
        cp.wait_send()


def hand_out(blocks, tile, o1, o2, o3, ot):
    o1[...] = blocks[0]
    o2[...] = blocks[1]
    o3[...] = blocks[2]
    for i, n in enumerate((0, 3, 5, 1, 2, 4)):
        ot[i] = tile[:, 16 * n:16 * n + 16]


def body(ancestor_inverse, panel_one, panel_two, panel_three, couplings, diag_terms, list_two, list_three):
    any_spec = pl.BlockSpec(memory_space=pl.ANY)
    vm = pl.BlockSpec(memory_space=pltpu.VMEM)
    dma = pltpu.SemaphoreType.DMA
    blocks, tile = pl.pallas_call(
        kernel,
        out_shape=(
            jax.ShapeDtypeStruct((3, ROWS, W), F32),
            jax.ShapeDtypeStruct((8, 128), F32),
        ),
        in_specs=[any_spec] * 6 + [vm] * 2,
        out_specs=(vm,) * 2,
        scratch_shapes=[
            pltpu.VMEM((1024, 512), F32),
            pltpu.VMEM((3, W, W), BF16),
            pltpu.VMEM((3, W, W), F32),
            pltpu.VMEM((16, 2, 32, 512), BF16),
            pltpu.VMEM((16, 2, 32, 512), BF16),
            pltpu.VMEM((16, 3, ROWS, W), BF16),
            pltpu.VMEM((3, 16, ROWS, W), BF16),
            pltpu.VMEM((4, 4, ROWS, 768), F32),
            pltpu.VMEM((4, 4, ROWS, 768), F32),
            pltpu.VMEM((4, 4, ROWS, 768), F32),
            *[pltpu.VMEM((6, 2, ROWS, hi - lo), F32) for lo, hi in STREAMS],
            *[pltpu.VMEM((3, ROWS, hi - lo), F32) for lo, hi in STREAMS],
            *[pltpu.VMEM((4, ROWS, hi - lo), F32) for lo, hi in STREAMS],
            pltpu.VMEM((ROWS, 768), F32),
            pltpu.VMEM((6, 4, 4, 2, 8, W), F32),
            pltpu.VMEM((6, 4, 4, 8, W), F32),
            *[pltpu.VMEM((6, 3, 2, 8, hi - lo), F32) for _, lo, hi, _ in GROUPS],
            *[pltpu.VMEM((3, 3, 8, hi - lo), F32) for _, lo, hi, _ in GROUPS],
            *[pltpu.VMEM((3, 4, 8, hi - lo), F32) for _, lo, hi, _ in GROUPS],
            pltpu.VMEM((16, 8, 128), F32),
            pltpu.VMEM((15, 8, 128), F32),
            dma((6,)), pltpu.SemaphoreType.REGULAR,
            dma((24,)), dma((24,)), dma((21,)), dma((21,)), dma((48,)), dma((48,)), dma((3,)), dma((3,)),
            dma((24,)), dma((24,)), dma((12,)), dma((12,)),
            dma((2,)), dma((2,)), dma((18,)), dma((18,)), dma((9,)), dma((9,)), dma((15,)), dma((15,)),
        ],
        compiler_params=pltpu.CompilerParams(
            collective_id=0, has_side_effects=True, vmem_limit_bytes=56 << 20
        ),
        name="chain_inverse",
    )(
        ancestor_inverse, panel_one, panel_two, panel_three, couplings, diag_terms,
        list_two.reshape(1, -1), list_three.reshape(1, -1),
    )
    *inverses, small = pl.pallas_call(
        hand_out,
        out_shape=(jax.ShapeDtypeStruct((ROWS, W), F32),) * 3 + (jax.ShapeDtypeStruct((6, 8, 16), F32),),
        in_specs=[vm] * 2,
        out_specs=(vm,) * 4,
        name="hand_out",
    )(blocks, tile)
    return (*inverses, jnp.swapaxes(small, 1, 2))


def solution(mesh):
    rows = P(("row", "col"), None)
    return jax.shard_map(
        body,
        mesh=mesh,
        in_specs=(P("row", "col"), rows, rows, rows, P(), P(), P(), P()),
        out_specs=(rows, rows, rows, P(None, "row", "col")),
        check_vma=False,
    )
```

```python
import functools

import jax
import jax.numpy as jnp
from jax import lax
from jax.experimental import pallas as pl
from jax.experimental.pallas import tpu as pltpu
from jax.sharding import PartitionSpec as P

MESH = pl.DeviceIdType.MESH
F32 = jnp.float32
BF16 = jnp.bfloat16
NZ, NK, W, ROWS = 16, 16, 256, 32
REACH = {1: 8, -1: 7}
GROUPS = (
    (0, 3, 0, 256, True), (3, 2, 0, 128, True), (3, 2, 128, 256, False), (5, 1, 0, 128, True), (5, 1, 128, 256, False),
)
SETS = ((0, 3), (3, 2), (5, 1))
STREAMS = ((0, 256), (256, 512), (512, 640), (640, 768))


def halves(v):
    hi = v.astype(BF16)
    return hi, (v - hi.astype(F32)).astype(BF16)


def mm(v, c):
    hi, lo = halves(v)
    return jnp.dot(hi, c, preferred_element_type=F32) + jnp.dot(lo, c, preferred_element_type=F32)


def turned_dot(a, b):
    return lax.dot_general(a, b, (((0,), (0,)), ((), ())), preferred_element_type=F32)


def tmc(v, c):
    hi, lo = halves(v)
    return turned_dot(hi, c) + turned_dot(lo, c)


def ctm(c, v):
    hi, lo = halves(v)
    return turned_dot(c, hi) + turned_dot(c, lo)


def tmm(a, b):
    ah, al = halves(a)
    bh, bl = halves(b)
    return turned_dot(jnp.concatenate([ah, al, ah], axis=0), jnp.concatenate([bh, bh, bl], axis=0))


def keep_of(lines, block):
    return jnp.max(jnp.where(lines == block, 1.0, 0.0).astype(F32))


def kernel(
    a_hbm, p1, p2, p3, coup_hbm, diag_hbm, l2, l3,
    o, ot,
    a_vm, coup, diag, ahi, alo, ring, fbuf, pown, ppar, prec,
    rec0, rec1, rec2, rec3, far0, far1, far2, far3, mid0, mid1, mid2, mid3, ysum,
    phi, qrec, zsend, zrec, gr,
    lsem, in_sem, up_s, up_r, dn_s, dn_r, f_s, f_r, pr_s, pr_r,
    rel_s, rel_r, far_s, far_r,
    q_s, q_r, g_s, g_r, gf_s, gf_r, z_s, z_r,
):
    z = lax.axis_index("row")
    c = lax.axis_index("col")
    e = c % 2
    k = c // 2
    y = k // 4
    x = k % 4
    half = y // 2
    partner = k * 2 + (1 - e)

    def col_of(yy, xx):
        return (yy * 4 + xx) * 2 + e

    own = []
    for i, p in enumerate((p1, p2, p3)):
        cp = pltpu.make_async_copy(p, ring.at[z, i], lsem.at[1 + i])
        cp.start()
        own.append(cp)
    acopy = pltpu.make_async_copy(a_hbm, a_vm, lsem.at[0])
    ccopy = pltpu.make_async_copy(coup_hbm, coup, lsem.at[4])
    dcopy = pltpu.make_async_copy(diag_hbm, diag, lsem.at[5])
    for cp in (acopy, ccopy, dcopy):
        cp.start()

    barrier = pltpu.get_barrier_semaphore()
    line = [partner]
    cross = []
    for d in (1, 2, 3):
        for ee in (0, 1):
            line.append((y * 4 + (x + d) % 4) * 2 + ee)
            cross.append(((y + d) % 4 * 4 + x) * 2 + ee)
    for to in line + cross:
        pl.semaphore_signal(barrier, inc=1, device_id=(z, to), device_id_type=MESH)
    for d in (1, 2, 14, 15):
        pl.semaphore_signal(barrier, inc=1, device_id=((z + d) % 16, c), device_id_type=MESH)
    for cp in own:
        cp.wait()
    pl.semaphore_wait(barrier, 17)
    for to in cross:
        pl.semaphore_signal(in_sem, inc=1, device_id=(z, to), device_id_type=MESH)

    slot = (k % 8) * 2 + e

    def hop(item, dist, step, q, way):
        send, recv = (up_s, up_r) if way > 0 else (dn_s, dn_r)
        part = ring.at[item, q]
        n = 3 * (dist + step - 1) + q
        return pltpu.make_async_remote_copy(
            src_ref=part, dst_ref=part, send_sem=send.at[n], recv_sem=recv.at[n],
            device_id=((z + 16 + way * step) % 16, c), device_id_type=MESH)

    def item_at(dist, way):
        return (z + 16 - way * dist) % 16

    def push(dist, q, way):
        for step in (2, 1):
            if dist + step <= REACH[way]:
                hop(item_at(dist, way), dist, step, q, way).start()

    def landed(dist, q, way):
        hop(item_at(dist, way), dist - 1, 1, q, way).wait_recv()

    def plane_copy(item, q):
        return pltpu.make_async_remote_copy(
            src_ref=ring.at[item, q], dst_ref=fbuf.at[q, slot],
            send_sem=f_s.at[3 * item + q], recv_sem=f_r.at[3 * slot + q],
            device_id=(z, item * 2 + half), device_id_type=MESH)

    def spread(item, q):
        mine = (item * 2 + half) == c

        @pl.when(mine)
        def _():
            pltpu.make_async_copy(ring.at[item, q], fbuf.at[q, slot], f_r.at[3 * slot + q]).start()

        @pl.when(jnp.logical_not(mine))
        def _():
            plane_copy(item, q).start()

    for q in range(3):
        for way in (1, -1):
            push(0, q, way)
    pl.semaphore_wait(in_sem, 6)
    for q in range(3):
        spread(z, q)
    def level(dist):
        for at in (dist, dist - 1):
            for q in range(3):
                for way in (1, -1):
                    if at <= REACH[way]:
                        landed(at, q, way)
                        if at == dist:
                            push(at, q, way)
                        spread(item_at(at, way), q)

    lines2 = l2[...]
    lines3 = l3[...]
    block = (z * 32 + c) // 8
    keep2 = keep_of(lines2, block)
    keep3 = keep_of(lines3, block)
    level(2)
    acopy.wait()

    @pl.loop(0, 16)
    def _(i):
        hi, lo = halves(a_vm[pl.ds(pl.multiple_of(i * 64, 64), 64), :])
        ahi[i] = hi.reshape(2, 32, 512)
        alo[i] = lo.reshape(2, 32, 512)

    level(4)
    ccopy.wait()
    dcopy.wait()
    c0, c1, c2 = coup[0], coup[1], coup[2]
    first = jnp.where((z == 0) & (c == 0), 1.0, 0.0).astype(F32)
    g1 = diag[0]
    h21 = -mm(g1, c0)
    g2 = diag[1] - ctm(c0, h21)
    level(6)
    h31 = -(mm(g1, c1) + mm(h21, c2))
    h32 = -(tmc(h21, c1) + mm(g2, c2))
    g3 = diag[2] - ctm(c1, h31) - ctm(c2, h32)
    for i, v in enumerate((g1, h21, h31, g2, h32, g3)):
        phi[i] = (v.T * first).reshape(4, 4, 2, 8, W)
    f1 = ring[z, 0].astype(F32)
    f2 = ring[z, 1].astype(F32) * keep2
    f3 = ring[z, 2].astype(F32) * keep3
    b = mm(f1, c0)
    g = mm(f1, c1)
    h = mm(f2, c2)
    q_ = mm(b, c2)
    level(8)

    def arrived(q):
        for i in range(16):
            pltpu.make_async_copy(ring.at[i, q], fbuf.at[q, i], f_r.at[3 * i + q]).wait()
        if q:
            lines = lines2 if q == 1 else lines3
            for j in range(2):
                s8 = slice(8 * j, 8 * j + 8)
                fbuf[q, s8] = (fbuf[q, s8].astype(F32) * keep_of(lines, 2 * c + j)).astype(BF16)

    def part(side, q):
        f = fbuf[q].reshape(512, W)
        out = jnp.dot(ahi[:, side].reshape(512, 512), f, preferred_element_type=F32)
        out = out + jnp.dot(alo[:, side].reshape(512, 512), f, preferred_element_type=F32)
        return out.reshape(4, 4, ROWS, W)

    def panel(q):
        return pl.ds(q * W, W)

    pair = []

    def to_partner(q):
        ppar[:, :, :, panel(q)] = part(1 - e, q)
        cp = pltpu.make_async_remote_copy(
            src_ref=ppar.at[:, :, :, panel(q)], dst_ref=prec.at[:, :, :, panel(q)],
            send_sem=pr_s.at[q], recv_sem=pr_r.at[q], device_id=(z, partner), device_id_type=MESH)
        cp.start()
        pair.append(cp)

    def from_partner(q):
        pair[q].wait_recv()
        pown[:, :, :, panel(q)] += prec[:, :, :, panel(q)]

    def exchange(src, rec, send, recv, d, to, n=0):
        cp = pltpu.make_async_remote_copy(
            src_ref=src, dst_ref=rec.at[d - 1], send_sem=send.at[n + d - 1], recv_sem=recv.at[n + d - 1],
            device_id=(z, to), device_id_type=MESH)
        cp.start()
        return cp

    def relay(view, rec, send, recv, p, right, left, base=0):
        def go(ref, n, to):
            cp = pltpu.make_async_remote_copy(
                src_ref=ref, dst_ref=rec.at[n], send_sem=send.at[base + n], recv_sem=recv.at[base + n],
                device_id=(z, to), device_id_type=MESH)
            cp.start()
            return cp

        far, after, before = (p + 2) % 4, (p + 1) % 4, (p + 3) % 4
        cps = [go(view(far, 0), 0, right), go(view(far, 1), 1, left),
               go(view(after, 1), 2, right), go(view(before, 0), 3, left)]

        def middle():
            for n, q, h, to in ((0, after, 0, right), (1, before, 1, left)):
                cps[n].wait_recv()
                ref = view(q, h)
                ref[...] += rec[n]
                cps.append(go(ref, 4 + n, to))

        def finish():
            for cp in cps[2:]:
                cp.wait_recv()
            return view(p, 0)[...] + rec[3] + rec[4], view(p, 1)[...] + rec[2] + rec[5]

        return cps, middle, finish

    xn, yn = [col_of(y, (x + d) % 4) for d in (1, 3)], [col_of((y + d) % 4, x) for d in (1, 3)]
    recs, mids, fars = (rec0, rec1, rec2, rec3), (mid0, mid1, mid2, mid3), (far0, far1, far2, far3)
    mid_of, end_of, second = [], [], [[], [], [], []]

    def open_stream(n):
        lo, hi = STREAMS[n]
        if n % 2 == 0:
            r = relay(lambda q, h: pown.at[2 * h:2 * h + 2, q, :, lo:hi], recs[n], rel_s, rel_r, x, *xn, base=6 * n)
        else:
            r = relay(lambda q, h: pown.at[q, 2 * h:2 * h + 2, :, lo:hi], recs[n], rel_s, rel_r, y, *yn, base=6 * n)
        mid_of.append((r[1], r[0]))
        end_of.append(r[2])

    def second_stage(n):
        mids[n][0:2], mids[n][2:4] = end_of[n]()
        for d in (2, 1, 3):
            if n % 2 == 0:
                src, to = mids[n].at[(y + d) % 4], col_of((y + d) % 4, x)
            else:
                src, to = mids[n].at[(x + d) % 4], col_of(y, (x + d) % 4)
            second[n].append(exchange(src, fars[n], far_s, far_r, d, to, n=3 * n))

    def close_stream(n):
        for cp in second[n]:
            cp.wait_recv()
        lo, hi = STREAMS[n]
        own_part = mids[n][y if n % 2 == 0 else x]
        ysum[:, lo:hi] = own_part + fars[n][0] + fars[n][1] + fars[n][2]

    arrived(0)
    to_partner(0)
    pown[:, :, :, panel(0)] = part(e, 0)
    arrived(1)
    to_partner(1)
    from_partner(0)
    open_stream(0)
    pown[:, :, :, panel(1)] = part(e, 1)
    arrived(2)
    to_partner(2)
    from_partner(1)
    open_stream(1)
    pown[:, :, :, panel(2)] = part(e, 2)
    mid_of[0][0]()
    from_partner(2)
    open_stream(2)
    open_stream(3)
    mid_of[1][0]()
    second_stage(0)
    mid_of[2][0]()
    mid_of[3][0]()
    second_stage(1)
    second_stage(2)
    second_stage(3)
    def add(i, right, left):
        val = tmm(jnp.concatenate(right, axis=0), jnp.concatenate(left, axis=0))
        phi[i] += val.reshape(4, 4, 2, 8, W)

    def pair_terms(n):
        at = pl.ds(*SETS[n])
        cp = pltpu.make_async_remote_copy(
            src_ref=phi.at[at, :, :, 1 - e], dst_ref=qrec.at[at],
            send_sem=q_s.at[n], recv_sem=q_r.at[n], device_id=(z, partner), device_id_type=MESH)
        cp.start()
        return cp

    group_rec, group_far, group_mid = gr[0::3], gr[1::3], gr[2::3]
    ga_rec, ga_mid = group_rec[0], group_mid[0]

    def met(n):
        terms[n].wait_recv()
        at = slice(SETS[n][0], SETS[n][0] + SETS[n][1])
        qrec[at] += phi[at, :, :, e]

    def spots(n, first_stage):
        along_x = GROUPS[n][4] == first_stage
        out = [((x + d) % 4, col_of(y, (x + d) % 4)) if along_x else ((y + d) % 4, col_of((y + d) % 4, x))
               for d in range(4)]
        return out

    def slab(n, q):
        blk, nb, lo, hi, xfirst = GROUPS[n]
        at = pl.ds(blk, nb)
        return qrec.at[at, :, q, :, lo:hi] if xfirst else qrec.at[at, q, :, :, lo:hi]

    def open_direct(n):
        to = spots(n, True)
        return [exchange(slab(n, to[d][0]), group_rec[n], g_s, g_r, d, to[d][1], n=3 + 3 * n) for d in (2, 1, 3)]

    def second_group(n):
        to = spots(n, False)
        return [exchange(group_mid[n].at[:, to[d][0]], group_far[n], gf_s, gf_r, d, to[d][1], n=3 * n)
                for d in (2, 1, 3)]

    def turn_direct(n, cps):
        for cp in cps:
            cp.wait_recv()
        rec = group_rec[n]
        group_mid[n][...] = slab(n, x if GROUPS[n][4] else y)[...] + rec[0] + rec[1] + rec[2]
        return second_group(n)

    def close_group(n, cps):
        for cp in cps:
            cp.wait_recv()
        far = group_far[n]
        return group_mid[n][:, y if GROUPS[n][4] else x] + far[0] + far[1] + far[2]

    def pack(blk, val):
        for zz in range(16):
            for i in range(val.shape[0]):
                at = 16 * (blk + i)
                zsend[zz, :, at:at + 16] = val[i][:, 16 * zz:16 * zz + 16]

    terms = []
    close_stream(0)
    y1 = ysum[:, 0:W]
    a = mm(y1, c0)
    w = mm(y1, c1)
    u = mm(a, c2)
    add(0, [y1], [f1])
    add(1, [f2, -a], [y1, f1])
    add(2, [f3 - h, u - w], [y1, f1])
    terms.append(pair_terms(0))
    o[0] = -y1
    close_stream(1)
    y2 = (ysum[:, W:2 * W] - a) * keep2
    v = mm(y2, c2)
    add(3, [y2, -f2, a], [f2, a, b])
    add(4, [f3, -(w + v), g + h, -u], [y2, f2, a, b])
    terms.append(pair_terms(1))
    o[1] = -y2
    met(0)
    wide, wide_mid, wide_end = relay(
        lambda q, hh: qrec.at[0:3, 2 * hh:2 * hh + 2, q], ga_rec, g_s, g_r, x, *xn)
    for zz in range(16):
        zsend[zz, :, 96:128] = jnp.zeros((8, 32), F32)
    close_stream(2)
    close_stream(3)
    y3 = (ysum[:, 2 * W:3 * W] - w - v) * keep3
    add(5, [y3, h - f3, w - u, -f3, w + v, -(g + h), u], [f3, w, g, v, h, u, q_])
    terms.append(pair_terms(2))
    o[2] = -y3
    met(1)
    firsts, lasts = {}, {}
    for n in (1, 2):
        firsts[n] = open_direct(n)
    wide_mid()
    met(2)
    for n in (3, 4):
        firsts[n] = open_direct(n)
    ga_mid[:, 0:2], ga_mid[:, 2:4] = wide_end()
    lasts[0] = second_group(0)
    for n in (1, 2, 3, 4):
        lasts[n] = turn_direct(n, firsts[n])
    pack(0, close_group(0, lasts[0]))
    for n, blk in ((1, 3), (3, 5)):
        left, right = close_group(n, lasts[n]), close_group(n + 1, lasts[n + 1])
        pack(blk, jnp.concatenate([left, right], axis=2))

    zc = []
    for d in (8, 7, 9, 6, 10, 5, 11, 4, 12, 3, 13, 2, 14, 1, 15):
        to = (z + d) % 16
        cp = pltpu.make_async_remote_copy(
            src_ref=zsend.at[to], dst_ref=zrec.at[d - 1], send_sem=z_s.at[d - 1], recv_sem=z_r.at[d - 1],
            device_id=(to, c), device_id_type=MESH)
        cp.start()
        zc.append(cp)
    for cp in zc:
        cp.wait_recv()
    tile = zsend[z]
    for d in range(15):
        tile = tile + zrec[d]
    ot[...] = tile

    for way in (1, -1):
        for dist in range(1, REACH[way] + 1):
            for q in range(3):
                hop(z, dist - 1, 1, q, way).wait_send()
    for i in range(16):
        @pl.when((i * 2 + half) != c)
        def _():
            for q in range(3):
                plane_copy(i, q).wait_send()
    near = [cp for _, cps in mid_of for cp in cps]
    near += wide + [cp for n in firsts for cp in firsts[n]] + [cp for n in lasts for cp in lasts[n]]
    for cp in pair + near + second[0] + second[1] + second[2] + second[3] + terms + zc:
        cp.wait_send()


def hand_out(blocks, tile, o1, o2, o3, ot):
    o1[...] = blocks[0]
    o2[...] = blocks[1]
    o3[...] = blocks[2]
    for i, n in enumerate((0, 3, 5, 1, 2, 4)):
        ot[i] = tile[:, 16 * n:16 * n + 16]


def body(ancestor_inverse, panel_one, panel_two, panel_three, couplings, diag_terms, list_two, list_three):
    any_spec = pl.BlockSpec(memory_space=pl.ANY)
    vm = pl.BlockSpec(memory_space=pltpu.VMEM)
    dma = pltpu.SemaphoreType.DMA
    blocks, tile = pl.pallas_call(
        kernel,
        out_shape=(
            jax.ShapeDtypeStruct((3, ROWS, W), F32),
            jax.ShapeDtypeStruct((8, 128), F32),
        ),
        in_specs=[any_spec] * 6 + [vm] * 2,
        out_specs=(vm,) * 2,
        scratch_shapes=[
            pltpu.VMEM((1024, 512), F32),
            pltpu.VMEM((3, W, W), BF16),
            pltpu.VMEM((3, W, W), F32),
            pltpu.VMEM((16, 2, 32, 512), BF16),
            pltpu.VMEM((16, 2, 32, 512), BF16),
            pltpu.VMEM((16, 3, ROWS, W), BF16),
            pltpu.VMEM((3, 16, ROWS, W), BF16),
            pltpu.VMEM((4, 4, ROWS, 768), F32),
            pltpu.VMEM((4, 4, ROWS, 768), F32),
            pltpu.VMEM((4, 4, ROWS, 768), F32),
            *[pltpu.VMEM((6, 2, ROWS, hi - lo), F32) for lo, hi in STREAMS],
            *[pltpu.VMEM((3, ROWS, hi - lo), F32) for lo, hi in STREAMS],
            *[pltpu.VMEM((4, ROWS, hi - lo), F32) for lo, hi in STREAMS],
            pltpu.VMEM((ROWS, 768), F32),
            pltpu.VMEM((6, 4, 4, 2, 8, W), F32),
            pltpu.VMEM((6, 4, 4, 8, W), F32),
            pltpu.VMEM((16, 8, 128), F32),
            pltpu.VMEM((15, 8, 128), F32),
            [pltpu.VMEM(shape, F32) for n, (_, nb, lo, hi, _) in enumerate(GROUPS) for shape in (
                (3, nb, 4, 8, hi - lo) if n else (6, nb, 2, 8, hi - lo), (3, nb, 8, hi - lo), (nb, 4, 8, hi - lo))],
            dma((6,)), pltpu.SemaphoreType.REGULAR,
            dma((24,)), dma((24,)), dma((21,)), dma((21,)), dma((48,)), dma((48,)), dma((3,)), dma((3,)),
            dma((24,)), dma((24,)), dma((12,)), dma((12,)),
            dma((3,)), dma((3,)), dma((18,)), dma((18,)), dma((15,)), dma((15,)), dma((15,)), dma((15,)),
        ],
        compiler_params=pltpu.CompilerParams(
            collective_id=0, has_side_effects=True, vmem_limit_bytes=56 << 20
        ),
        name="chain_inverse",
    )(
        ancestor_inverse, panel_one, panel_two, panel_three, couplings, diag_terms,
        list_two.reshape(1, -1), list_three.reshape(1, -1),
    )
    *inverses, small = pl.pallas_call(
        hand_out,
        out_shape=(jax.ShapeDtypeStruct((ROWS, W), F32),) * 3 + (jax.ShapeDtypeStruct((6, 8, 16), F32),),
        in_specs=[vm] * 2,
        out_specs=(vm,) * 4,
        name="hand_out",
    )(blocks, tile)
    return (*inverses, jnp.swapaxes(small, 1, 2))


def solution(mesh):
    rows = P(("row", "col"), None)
    return jax.shard_map(
        body,
        mesh=mesh,
        in_specs=(P("row", "col"), rows, rows, rows, P(), P(), P(), P()),
        out_specs=(rows, rows, rows, P(None, "row", "col")),
        check_vma=False,
    )
```

```python
import functools

import jax
import jax.numpy as jnp
from jax import lax
from jax.experimental import pallas as pl
from jax.experimental.pallas import tpu as pltpu
from jax.sharding import PartitionSpec as P

MESH = pl.DeviceIdType.MESH
F32 = jnp.float32
BF16 = jnp.bfloat16
NZ, NK, W, ROWS = 16, 16, 256, 32
REACH = {1: 8, -1: 7}
GROUPS = (
    (0, 3, 0, 256, True), (3, 2, 0, 128, True), (3, 2, 128, 256, False), (5, 1, 0, 128, True), (5, 1, 128, 256, False),
)
SETS = ((0, 3), (3, 2), (5, 1))
STREAMS = ((0, 256), (256, 512), (512, 640), (640, 768))


def halves(v):
    hi = v.astype(BF16)
    return hi, (v - hi.astype(F32)).astype(BF16)


def mm(v, c):
    hi, lo = halves(v)
    return jnp.dot(hi, c, preferred_element_type=F32) + jnp.dot(lo, c, preferred_element_type=F32)


def turned_dot(a, b):
    return lax.dot_general(a, b, (((0,), (0,)), ((), ())), preferred_element_type=F32)


def tmc(v, c):
    hi, lo = halves(v)
    return turned_dot(hi, c) + turned_dot(lo, c)


def ctm(c, v):
    hi, lo = halves(v)
    return turned_dot(c, hi) + turned_dot(c, lo)


def tmm(a, b):
    ah, al = halves(a)
    bh, bl = halves(b)
    return turned_dot(jnp.concatenate([ah, al, ah], axis=0), jnp.concatenate([bh, bh, bl], axis=0))


def keep_of(lines, block):
    return jnp.max(jnp.where(lines == block, 1.0, 0.0).astype(F32))


def kernel(
    a_hbm, p1, p2, p3, coup_hbm, diag_hbm, l2, l3,
    o, ot,
    a_vm, coup, diag, ahi, alo, ring, fbuf, pown, ppar, prec,
    rec0, rec1, rec2, rec3, far0, far1, far2, far3, mid0, mid1, mid2, mid3, ysum,
    phi, qrec, zsend, zrec, gr,
    lsem, in_sem, up_s, up_r, dn_s, dn_r, f_s, f_r, pr_s, pr_r,
    rel_s, rel_r, far_s, far_r,
    q_s, q_r, g_s, g_r, gf_s, gf_r, z_s, z_r,
):
    z = lax.axis_index("row")
    c = lax.axis_index("col")
    e = c % 2
    k = c // 2
    y = k // 4
    x = k % 4
    half = y // 2
    partner = k * 2 + (1 - e)

    def col_of(yy, xx):
        return (yy * 4 + xx) * 2 + e

    own = []
    for i, p in enumerate((p1, p2, p3)):
        cp = pltpu.make_async_copy(p, ring.at[z, i], lsem.at[1 + i])
        cp.start()
        own.append(cp)
    acopy = pltpu.make_async_copy(a_hbm, a_vm, lsem.at[0])
    ccopy = pltpu.make_async_copy(coup_hbm, coup, lsem.at[4])
    dcopy = pltpu.make_async_copy(diag_hbm, diag, lsem.at[5])
    for cp in (acopy, ccopy, dcopy):
        cp.start()

    barrier = pltpu.get_barrier_semaphore()
    line = [partner]
    cross = []
    for d in (1, 2, 3):
        for ee in (0, 1):
            line.append((y * 4 + (x + d) % 4) * 2 + ee)
            cross.append(((y + d) % 4 * 4 + x) * 2 + ee)
    for to in line + cross:
        pl.semaphore_signal(barrier, inc=1, device_id=(z, to), device_id_type=MESH)
    for d in (1, 2, 14, 15):
        pl.semaphore_signal(barrier, inc=1, device_id=((z + d) % 16, c), device_id_type=MESH)
    for cp in own:
        cp.wait()
    pl.semaphore_wait(barrier, 17)
    for to in cross:
        pl.semaphore_signal(in_sem, inc=1, device_id=(z, to), device_id_type=MESH)

    slot = (k % 8) * 2 + e

    def hop(item, dist, step, q, way):
        send, recv = (up_s, up_r) if way > 0 else (dn_s, dn_r)
        part = ring.at[item, q]
        n = 3 * (dist + step - 1) + q
        return pltpu.make_async_remote_copy(
            src_ref=part, dst_ref=part, send_sem=send.at[n], recv_sem=recv.at[n],
            device_id=((z + 16 + way * step) % 16, c), device_id_type=MESH)

    def item_at(dist, way):
        return (z + 16 - way * dist) % 16

    def push(dist, q, way):
        for step in (2, 1):
            if dist + step <= REACH[way]:
                hop(item_at(dist, way), dist, step, q, way).start()

    def landed(dist, q, way):
        hop(item_at(dist, way), dist - 1, 1, q, way).wait_recv()

    def plane_copy(item, q):
        return pltpu.make_async_remote_copy(
            src_ref=ring.at[item, q], dst_ref=fbuf.at[q, slot],
            send_sem=f_s.at[3 * item + q], recv_sem=f_r.at[3 * slot + q],
            device_id=(z, item * 2 + half), device_id_type=MESH)

    def spread(item, q):
        mine = (item * 2 + half) == c

        @pl.when(mine)
        def _():
            pltpu.make_async_copy(ring.at[item, q], fbuf.at[q, slot], f_r.at[3 * slot + q]).start()

        @pl.when(jnp.logical_not(mine))
        def _():
            plane_copy(item, q).start()

    for q in range(3):
        for way in (1, -1):
            push(0, q, way)
    pl.semaphore_wait(in_sem, 6)
    for q in range(3):
        spread(z, q)
    def level(dist):
        for at in (dist, dist - 1):
            for q in range(3):
                for way in (1, -1):
                    if at <= REACH[way]:
                        landed(at, q, way)
                        if at == dist:
                            push(at, q, way)
                        spread(item_at(at, way), q)

    lines2 = l2[...]
    lines3 = l3[...]
    block = (z * 32 + c) // 8
    keep2 = keep_of(lines2, block)
    keep3 = keep_of(lines3, block)
    level(2)
    acopy.wait()

    @pl.loop(0, 16)
    def _(i):
        hi, lo = halves(a_vm[pl.ds(pl.multiple_of(i * 64, 64), 64), :])
        ahi[i] = hi.reshape(2, 32, 512)
        alo[i] = lo.reshape(2, 32, 512)

    level(4)
    ccopy.wait()
    dcopy.wait()
    c0, c1, c2 = coup[0], coup[1], coup[2]
    first = jnp.where((z == 0) & (c == 0), 1.0, 0.0).astype(F32)
    g1 = diag[0]
    h21 = -mm(g1, c0)
    g2 = diag[1] - ctm(c0, h21)
    level(6)
    h31 = -(mm(g1, c1) + mm(h21, c2))
    h32 = -(tmc(h21, c1) + mm(g2, c2))
    g3 = diag[2] - ctm(c1, h31) - ctm(c2, h32)
    for i, v in enumerate((g1, h21, h31, g2, h32, g3)):
        for side in range(2):
            phi[i, side] = (v.T * first).reshape(4, 4, 2, 8, W)[:, :, side]
    f1 = ring[z, 0].astype(F32)
    f2 = ring[z, 1].astype(F32) * keep2
    f3 = ring[z, 2].astype(F32) * keep3
    b = mm(f1, c0)
    g = mm(f1, c1)
    h = mm(f2, c2)
    q_ = mm(b, c2)
    level(8)

    def arrived(q):
        for i in range(16):
            pltpu.make_async_copy(ring.at[i, q], fbuf.at[q, i], f_r.at[3 * i + q]).wait()
        if q:
            lines = lines2 if q == 1 else lines3
            for j in range(2):
                s8 = slice(8 * j, 8 * j + 8)
                fbuf[q, s8] = (fbuf[q, s8].astype(F32) * keep_of(lines, 2 * c + j)).astype(BF16)

    def part(side, q):
        f = fbuf[q].reshape(512, W)
        out = jnp.dot(ahi[:, side].reshape(512, 512), f, preferred_element_type=F32)
        out = out + jnp.dot(alo[:, side].reshape(512, 512), f, preferred_element_type=F32)
        return out.reshape(4, 4, ROWS, W)

    def put(bufs, q, val):
        for n, (lo, hi) in enumerate(STREAMS):
            if q * W <= lo < (q + 1) * W:
                bufs[n][...] = val[:, :, :, lo - q * W:hi - q * W]

    pair = []

    def to_partner(q):
        put(ppar, q, part(1 - e, q))
        for n in ((0,), (1,), (2, 3))[q]:
            cp = pltpu.make_async_remote_copy(
                src_ref=ppar[n], dst_ref=prec[n],
                send_sem=pr_s.at[n], recv_sem=pr_r.at[n], device_id=(z, partner), device_id_type=MESH)
            cp.start()
            pair.append(cp)

    def from_partner(n):
        pair[n].wait_recv()
        pown[n][...] += prec[n][...]

    def exchange(src, rec, send, recv, d, to, n=0):
        cp = pltpu.make_async_remote_copy(
            src_ref=src, dst_ref=rec.at[d - 1], send_sem=send.at[n + d - 1], recv_sem=recv.at[n + d - 1],
            device_id=(z, to), device_id_type=MESH)
        cp.start()
        return cp

    def relay(view, rec, send, recv, p, right, left, base=0):
        def go(ref, n, to):
            cp = pltpu.make_async_remote_copy(
                src_ref=ref, dst_ref=rec.at[n], send_sem=send.at[base + n], recv_sem=recv.at[base + n],
                device_id=(z, to), device_id_type=MESH)
            cp.start()
            return cp

        far, after, before = (p + 2) % 4, (p + 1) % 4, (p + 3) % 4
        cps = [go(view(far, 0), 0, right), go(view(far, 1), 1, left),
               go(view(after, 1), 2, right), go(view(before, 0), 3, left)]

        def middle():
            for n, q, h, to in ((0, after, 0, right), (1, before, 1, left)):
                cps[n].wait_recv()
                ref = view(q, h)
                ref[...] += rec[n]
                cps.append(go(ref, 4 + n, to))

        def finish():
            for cp in cps[2:]:
                cp.wait_recv()
            return view(p, 0)[...] + rec[3] + rec[4], view(p, 1)[...] + rec[2] + rec[5]

        return cps, middle, finish

    xn, yn = [col_of(y, (x + d) % 4) for d in (1, 3)], [col_of((y + d) % 4, x) for d in (1, 3)]
    recs, mids, fars = (rec0, rec1, rec2, rec3), (mid0, mid1, mid2, mid3), (far0, far1, far2, far3)
    mid_of, end_of, second = [], [], [[], [], [], []]

    def open_stream(n):
        from_partner(n)
        if n % 2 == 0:
            r = relay(lambda q, h: pown[n].at[2 * h:2 * h + 2, q], recs[n], rel_s, rel_r, x, *xn, base=6 * n)
        else:
            r = relay(lambda q, h: pown[n].at[q, 2 * h:2 * h + 2], recs[n], rel_s, rel_r, y, *yn, base=6 * n)
        mid_of.append((r[1], r[0]))
        end_of.append(r[2])

    def second_stage(n):
        mids[n][0:2], mids[n][2:4] = end_of[n]()
        for d in (2, 1, 3):
            if n % 2 == 0:
                src, to = mids[n].at[(y + d) % 4], col_of((y + d) % 4, x)
            else:
                src, to = mids[n].at[(x + d) % 4], col_of(y, (x + d) % 4)
            second[n].append(exchange(src, fars[n], far_s, far_r, d, to, n=3 * n))

    def close_stream(n):
        for cp in second[n]:
            cp.wait_recv()
        lo, hi = STREAMS[n]
        own_part = mids[n][y if n % 2 == 0 else x]
        ysum[:, lo:hi] = own_part + fars[n][0] + fars[n][1] + fars[n][2]

    arrived(0)
    to_partner(0)
    put(pown, 0, part(e, 0))
    arrived(1)
    to_partner(1)
    open_stream(0)
    put(pown, 1, part(e, 1))
    arrived(2)
    to_partner(2)
    open_stream(1)
    put(pown, 2, part(e, 2))
    mid_of[0][0]()
    open_stream(2)
    open_stream(3)
    mid_of[1][0]()
    second_stage(0)
    mid_of[2][0]()
    mid_of[3][0]()
    second_stage(1)
    second_stage(2)
    second_stage(3)
    def add(i, right, left):
        val = tmm(jnp.concatenate(right, axis=0), jnp.concatenate(left, axis=0))
        for side in range(2):
            phi[i, side] += val.reshape(4, 4, 2, 8, W)[:, :, side]

    def pair_terms(n):
        at = pl.ds(*SETS[n])
        cp = pltpu.make_async_remote_copy(
            src_ref=phi.at[at, 1 - e], dst_ref=qrec.at[at],
            send_sem=q_s.at[n], recv_sem=q_r.at[n], device_id=(z, partner), device_id_type=MESH)
        cp.start()
        return cp

    group_rec, group_far, group_mid = gr[0::3], gr[1::3], gr[2::3]
    ga_rec, ga_mid = group_rec[0], group_mid[0]

    def met(n):
        terms[n].wait_recv()
        at = slice(SETS[n][0], SETS[n][0] + SETS[n][1])
        qrec[at] += phi[at, e]

    def spots(n, first_stage):
        along_x = GROUPS[n][4] == first_stage
        out = [((x + d) % 4, col_of(y, (x + d) % 4)) if along_x else ((y + d) % 4, col_of((y + d) % 4, x))
               for d in range(4)]
        return out

    def slab(n, q):
        blk, nb, lo, hi, xfirst = GROUPS[n]
        at = pl.ds(blk, nb)
        return qrec.at[at, :, q, :, lo:hi] if xfirst else qrec.at[at, q, :, :, lo:hi]

    def open_direct(n):
        to = spots(n, True)
        return [exchange(slab(n, to[d][0]), group_rec[n], g_s, g_r, d, to[d][1], n=3 + 3 * n) for d in (2, 1, 3)]

    def second_group(n):
        to = spots(n, False)
        return [exchange(group_mid[n].at[:, to[d][0]], group_far[n], gf_s, gf_r, d, to[d][1], n=3 * n)
                for d in (2, 1, 3)]

    def turn_direct(n, cps):
        for cp in cps:
            cp.wait_recv()
        rec = group_rec[n]
        group_mid[n][...] = slab(n, x if GROUPS[n][4] else y)[...] + rec[0] + rec[1] + rec[2]
        return second_group(n)

    def close_group(n, cps):
        for cp in cps:
            cp.wait_recv()
        far = group_far[n]
        return group_mid[n][:, y if GROUPS[n][4] else x] + far[0] + far[1] + far[2]

    def pack(blk, val):
        for zz in range(16):
            for i in range(val.shape[0]):
                at = 16 * (blk + i)
                zsend[zz, :, at:at + 16] = val[i][:, 16 * zz:16 * zz + 16]

    terms = []
    close_stream(0)
    y1 = ysum[:, 0:W]
    a = mm(y1, c0)
    w = mm(y1, c1)
    u = mm(a, c2)
    add(0, [y1], [f1])
    add(1, [f2, -a], [y1, f1])
    add(2, [f3 - h, u - w], [y1, f1])
    terms.append(pair_terms(0))
    o[0] = -y1
    close_stream(1)
    y2 = (ysum[:, W:2 * W] - a) * keep2
    v = mm(y2, c2)
    add(3, [y2, -f2, a], [f2, a, b])
    add(4, [f3, -(w + v), g + h, -u], [y2, f2, a, b])
    terms.append(pair_terms(1))
    o[1] = -y2
    met(0)
    wide, wide_mid, wide_end = relay(
        lambda q, hh: qrec.at[0:3, 2 * hh:2 * hh + 2, q], ga_rec, g_s, g_r, x, *xn)
    for zz in range(16):
        zsend[zz, :, 96:128] = jnp.zeros((8, 32), F32)
    close_stream(2)
    close_stream(3)
    y3 = (ysum[:, 2 * W:3 * W] - w - v) * keep3
    add(5, [y3, h - f3, w - u, -f3, w + v, -(g + h), u], [f3, w, g, v, h, u, q_])
    terms.append(pair_terms(2))
    o[2] = -y3
    met(1)
    firsts, lasts = {}, {}
    for n in (1, 2):
        firsts[n] = open_direct(n)
    wide_mid()
    met(2)
    for n in (3, 4):
        firsts[n] = open_direct(n)
    ga_mid[:, 0:2], ga_mid[:, 2:4] = wide_end()
    lasts[0] = second_group(0)
    for n in (1, 2, 3, 4):
        lasts[n] = turn_direct(n, firsts[n])
    pack(0, close_group(0, lasts[0]))
    for n, blk in ((1, 3), (3, 5)):
        left, right = close_group(n, lasts[n]), close_group(n + 1, lasts[n + 1])
        pack(blk, jnp.concatenate([left, right], axis=2))

    zc = []
    for d in (8, 7, 9, 6, 10, 5, 11, 4, 12, 3, 13, 2, 14, 1, 15):
        to = (z + d) % 16
        cp = pltpu.make_async_remote_copy(
            src_ref=zsend.at[to], dst_ref=zrec.at[d - 1], send_sem=z_s.at[d - 1], recv_sem=z_r.at[d - 1],
            device_id=(to, c), device_id_type=MESH)
        cp.start()
        zc.append(cp)
    for cp in zc:
        cp.wait_recv()
    tile = zsend[z]
    for d in range(15):
        tile = tile + zrec[d]
    ot[...] = tile

    for way in (1, -1):
        for dist in range(1, REACH[way] + 1):
            for q in range(3):
                hop(z, dist - 1, 1, q, way).wait_send()
    for i in range(16):
        @pl.when((i * 2 + half) != c)
        def _():
            for q in range(3):
                plane_copy(i, q).wait_send()
    near = [cp for _, cps in mid_of for cp in cps]
    near += wide + [cp for n in firsts for cp in firsts[n]] + [cp for n in lasts for cp in lasts[n]]
    for cp in pair + near + second[0] + second[1] + second[2] + second[3] + terms + zc:
        cp.wait_send()


def hand_out(blocks, tile, o1, o2, o3, ot):
    o1[...] = blocks[0]
    o2[...] = blocks[1]
    o3[...] = blocks[2]
    for i, n in enumerate((0, 3, 5, 1, 2, 4)):
        ot[i] = tile[:, 16 * n:16 * n + 16]


def body(ancestor_inverse, panel_one, panel_two, panel_three, couplings, diag_terms, list_two, list_three):
    any_spec = pl.BlockSpec(memory_space=pl.ANY)
    vm = pl.BlockSpec(memory_space=pltpu.VMEM)
    dma = pltpu.SemaphoreType.DMA
    blocks, tile = pl.pallas_call(
        kernel,
        out_shape=(
            jax.ShapeDtypeStruct((3, ROWS, W), F32),
            jax.ShapeDtypeStruct((8, 128), F32),
        ),
        in_specs=[any_spec] * 6 + [vm] * 2,
        out_specs=(vm,) * 2,
        scratch_shapes=[
            pltpu.VMEM((1024, 512), F32),
            pltpu.VMEM((3, W, W), BF16),
            pltpu.VMEM((3, W, W), F32),
            pltpu.VMEM((16, 2, 32, 512), BF16),
            pltpu.VMEM((16, 2, 32, 512), BF16),
            pltpu.VMEM((16, 3, ROWS, W), BF16),
            pltpu.VMEM((3, 16, ROWS, W), BF16),
            *[[pltpu.VMEM((4, 4, ROWS, hi - lo), F32) for lo, hi in STREAMS]] * 3,
            *[pltpu.VMEM((6, 2, ROWS, hi - lo), F32) for lo, hi in STREAMS],
            *[pltpu.VMEM((3, ROWS, hi - lo), F32) for lo, hi in STREAMS],
            *[pltpu.VMEM((4, ROWS, hi - lo), F32) for lo, hi in STREAMS],
            pltpu.VMEM((ROWS, 768), F32),
            pltpu.VMEM((6, 2, 4, 4, 8, W), F32),
            pltpu.VMEM((6, 4, 4, 8, W), F32),
            pltpu.VMEM((16, 8, 128), F32),
            pltpu.VMEM((15, 8, 128), F32),
            [pltpu.VMEM(shape, F32) for n, (_, nb, lo, hi, _) in enumerate(GROUPS) for shape in (
                (3, nb, 4, 8, hi - lo) if n else (6, nb, 2, 8, hi - lo), (3, nb, 8, hi - lo), (nb, 4, 8, hi - lo))],
            dma((6,)), pltpu.SemaphoreType.REGULAR,
            dma((24,)), dma((24,)), dma((21,)), dma((21,)), dma((48,)), dma((48,)), dma((4,)), dma((4,)),
            dma((24,)), dma((24,)), dma((12,)), dma((12,)),
            dma((3,)), dma((3,)), dma((18,)), dma((18,)), dma((15,)), dma((15,)), dma((15,)), dma((15,)),
        ],
        compiler_params=pltpu.CompilerParams(
            collective_id=0, has_side_effects=True, vmem_limit_bytes=56 << 20
        ),
        name="chain_inverse",
    )(
        ancestor_inverse, panel_one, panel_two, panel_three, couplings, diag_terms,
        list_two.reshape(1, -1), list_three.reshape(1, -1),
    )
    *inverses, small = pl.pallas_call(
        hand_out,
        out_shape=(jax.ShapeDtypeStruct((ROWS, W), F32),) * 3 + (jax.ShapeDtypeStruct((6, 8, 16), F32),),
        in_specs=[vm] * 2,
        out_specs=(vm,) * 4,
        name="hand_out",
    )(blocks, tile)
    return (*inverses, jnp.swapaxes(small, 1, 2))


def solution(mesh):
    rows = P(("row", "col"), None)
    return jax.shard_map(
        body,
        mesh=mesh,
        in_specs=(P("row", "col"), rows, rows, rows, P(), P(), P(), P()),
        out_specs=(rows, rows, rows, P(None, "row", "col")),
        check_vma=False,
    )
```

```python
import functools

import jax
import jax.numpy as jnp
from jax import lax
from jax.experimental import pallas as pl
from jax.experimental.pallas import tpu as pltpu
from jax.sharding import PartitionSpec as P

MESH = pl.DeviceIdType.MESH
F32 = jnp.float32
BF16 = jnp.bfloat16
NZ, NK, W, ROWS = 16, 16, 256, 32
REACH = {1: 8, -1: 7}
GROUPS = (
    (0, 3, 0, 256, True), (3, 2, 0, 128, True), (3, 2, 128, 256, False), (5, 1, 0, 128, True), (5, 1, 128, 256, False),
)
SETS = ((0, 3), (3, 2))
STREAMS = ((0, 256), (256, 512), (512, 640), (640, 768))


def halves(v):
    hi = v.astype(BF16)
    return hi, (v - hi.astype(F32)).astype(BF16)


def mm(v, c):
    hi, lo = halves(v)
    return jnp.dot(hi, c, preferred_element_type=F32) + jnp.dot(lo, c, preferred_element_type=F32)


def turned_dot(a, b):
    return lax.dot_general(a, b, (((0,), (0,)), ((), ())), preferred_element_type=F32)


def tmc(v, c):
    hi, lo = halves(v)
    return turned_dot(hi, c) + turned_dot(lo, c)


def ctm(c, v):
    hi, lo = halves(v)
    return turned_dot(c, hi) + turned_dot(c, lo)


def tmm(a, b):
    ah, al = halves(a)
    bh, bl = halves(b)
    return turned_dot(jnp.concatenate([ah, al, ah], axis=0), jnp.concatenate([bh, bh, bl], axis=0))


def keep_of(lines, block):
    return jnp.max(jnp.where(lines == block, 1.0, 0.0).astype(F32))


def kernel(
    a_hbm, p1, p2, p3, coup_hbm, diag_hbm, l2, l3,
    o, ot,
    a_vm, coup, diag, ahi, alo, ring, fbuf, pown, ppar, prec,
    rec0, rec1, rec2, rec3, far0, far1, far2, far3, mid0, mid1, mid2, mid3, ysum,
    phi, qrec, zsend, zrec, gr, o_vm,
    lsem, o_sem, in_sem, up_s, up_r, dn_s, dn_r, f_s, f_r, pr_s, pr_r,
    rel_s, rel_r, far_s, far_r,
    q_s, q_r, last_s, last_r, g_s, g_r, gf_s, gf_r, z_s, z_r,
):
    z = lax.axis_index("row")
    c = lax.axis_index("col")
    e = c % 2
    k = c // 2
    y = k // 4
    x = k % 4
    half = y // 2
    partner = k * 2 + (1 - e)

    def col_of(yy, xx):
        return (yy * 4 + xx) * 2 + e

    own = []
    for i, p in enumerate((p1, p2, p3)):
        cp = pltpu.make_async_copy(p, ring.at[z, i], lsem.at[1 + i])
        cp.start()
        own.append(cp)
    acopy = pltpu.make_async_copy(a_hbm, a_vm, lsem.at[0])
    ccopy = pltpu.make_async_copy(coup_hbm, coup, lsem.at[4])
    dcopy = pltpu.make_async_copy(diag_hbm, diag, lsem.at[5])
    for cp in (acopy, ccopy, dcopy):
        cp.start()

    barrier = pltpu.get_barrier_semaphore()
    line = [partner]
    cross = []
    for d in (1, 2, 3):
        for ee in (0, 1):
            line.append((y * 4 + (x + d) % 4) * 2 + ee)
            cross.append(((y + d) % 4 * 4 + x) * 2 + ee)
    for to in line + cross:
        pl.semaphore_signal(barrier, inc=1, device_id=(z, to), device_id_type=MESH)
    for d in (1, 2, 14, 15):
        pl.semaphore_signal(barrier, inc=1, device_id=((z + d) % 16, c), device_id_type=MESH)
    for cp in own:
        cp.wait()
    pl.semaphore_wait(barrier, 17)
    for to in cross:
        pl.semaphore_signal(in_sem, inc=1, device_id=(z, to), device_id_type=MESH)

    slot = (k % 8) * 2 + e

    def hop(item, dist, step, q, way):
        send, recv = (up_s, up_r) if way > 0 else (dn_s, dn_r)
        part = ring.at[item, q]
        n = 3 * (dist + step - 1) + q
        return pltpu.make_async_remote_copy(
            src_ref=part, dst_ref=part, send_sem=send.at[n], recv_sem=recv.at[n],
            device_id=((z + 16 + way * step) % 16, c), device_id_type=MESH)

    def item_at(dist, way):
        return (z + 16 - way * dist) % 16

    def push(dist, q, way):
        for step in (2, 1):
            if dist + step <= REACH[way]:
                hop(item_at(dist, way), dist, step, q, way).start()

    def landed(dist, q, way):
        hop(item_at(dist, way), dist - 1, 1, q, way).wait_recv()

    def plane_copy(item, q):
        return pltpu.make_async_remote_copy(
            src_ref=ring.at[item, q], dst_ref=fbuf.at[q, slot],
            send_sem=f_s.at[3 * item + q], recv_sem=f_r.at[3 * slot + q],
            device_id=(z, item * 2 + half), device_id_type=MESH)

    def spread(item, q):
        mine = (item * 2 + half) == c

        @pl.when(mine)
        def _():
            pltpu.make_async_copy(ring.at[item, q], fbuf.at[q, slot], f_r.at[3 * slot + q]).start()

        @pl.when(jnp.logical_not(mine))
        def _():
            plane_copy(item, q).start()

    for q in range(3):
        for way in (1, -1):
            push(0, q, way)
    pl.semaphore_wait(in_sem, 6)
    for q in range(3):
        spread(z, q)
    def level(dist):
        for at in (dist, dist - 1):
            for q in range(3):
                for way in (1, -1):
                    if at <= REACH[way]:
                        landed(at, q, way)
                        if at == dist:
                            push(at, q, way)
                        spread(item_at(at, way), q)

    lines2 = l2[...]
    lines3 = l3[...]
    block = (z * 32 + c) // 8
    keep2 = keep_of(lines2, block)
    keep3 = keep_of(lines3, block)
    level(2)
    acopy.wait()

    @pl.loop(0, 16)
    def _(i):
        hi, lo = halves(a_vm[pl.ds(pl.multiple_of(i * 64, 64), 64), :])
        ahi[i] = hi.reshape(2, 32, 512)
        alo[i] = lo.reshape(2, 32, 512)

    level(4)
    ccopy.wait()
    dcopy.wait()
    c0, c1, c2 = coup[0], coup[1], coup[2]
    first = jnp.where((z == 0) & (c == 0), 1.0, 0.0).astype(F32)
    g1 = diag[0]
    h21 = -mm(g1, c0)
    g2 = diag[1] - ctm(c0, h21)
    level(6)
    h31 = -(mm(g1, c1) + mm(h21, c2))
    h32 = -(tmc(h21, c1) + mm(g2, c2))
    g3 = diag[2] - ctm(c1, h31) - ctm(c2, h32)
    for i, v in enumerate((g1, h21, h31, g2, h32, g3)):
        for side in range(2):
            phi[i, side] = (v.T * first).reshape(4, 4, 2, 8, W)[:, :, side]
    f1 = ring[z, 0].astype(F32)
    f2 = ring[z, 1].astype(F32) * keep2
    f3 = ring[z, 2].astype(F32) * keep3
    b = mm(f1, c0)
    g = mm(f1, c1)
    h = mm(f2, c2)
    q_ = mm(b, c2)
    level(8)

    def arrived(q):
        for i in range(16):
            pltpu.make_async_copy(ring.at[i, q], fbuf.at[q, i], f_r.at[3 * i + q]).wait()
        if q:
            lines = lines2 if q == 1 else lines3
            for j in range(2):
                s8 = slice(8 * j, 8 * j + 8)
                fbuf[q, s8] = (fbuf[q, s8].astype(F32) * keep_of(lines, 2 * c + j)).astype(BF16)

    def part(side, q):
        f = fbuf[q].reshape(512, W)
        out = jnp.dot(ahi[:, side].reshape(512, 512), f, preferred_element_type=F32)
        out = out + jnp.dot(alo[:, side].reshape(512, 512), f, preferred_element_type=F32)
        return out.reshape(4, 4, ROWS, W)

    def put(bufs, q, val):
        for n, (lo, hi) in enumerate(STREAMS):
            if q * W <= lo < (q + 1) * W:
                bufs[n][...] = val[:, :, :, lo - q * W:hi - q * W]

    pair = []

    def to_partner(q):
        put(ppar, q, part(1 - e, q))
        for n in ((0,), (1,), (2, 3))[q]:
            cp = pltpu.make_async_remote_copy(
                src_ref=ppar[n], dst_ref=prec[n],
                send_sem=pr_s.at[n], recv_sem=pr_r.at[n], device_id=(z, partner), device_id_type=MESH)
            cp.start()
            pair.append(cp)

    def from_partner(n):
        pair[n].wait_recv()
        pown[n][...] += prec[n][...]

    def exchange(src, rec, send, recv, d, to, n=0):
        cp = pltpu.make_async_remote_copy(
            src_ref=src, dst_ref=rec.at[d - 1], send_sem=send.at[n + d - 1], recv_sem=recv.at[n + d - 1],
            device_id=(z, to), device_id_type=MESH)
        cp.start()
        return cp

    def relay(view, rec, send, recv, p, right, left, base=0):
        def go(ref, n, to):
            cp = pltpu.make_async_remote_copy(
                src_ref=ref, dst_ref=rec.at[n], send_sem=send.at[base + n], recv_sem=recv.at[base + n],
                device_id=(z, to), device_id_type=MESH)
            cp.start()
            return cp

        far, after, before = (p + 2) % 4, (p + 1) % 4, (p + 3) % 4
        cps = [go(view(far, 0), 0, right), go(view(far, 1), 1, left),
               go(view(after, 1), 2, right), go(view(before, 0), 3, left)]

        def middle():
            for n, q, h, to in ((0, after, 0, right), (1, before, 1, left)):
                cps[n].wait_recv()
                ref = view(q, h)
                ref[...] += rec[n]
                cps.append(go(ref, 4 + n, to))

        def finish():
            for cp in cps[2:]:
                cp.wait_recv()
            return view(p, 0)[...] + rec[3] + rec[4], view(p, 1)[...] + rec[2] + rec[5]

        return cps, middle, finish

    xn, yn = [col_of(y, (x + d) % 4) for d in (1, 3)], [col_of((y + d) % 4, x) for d in (1, 3)]
    recs, mids, fars = (rec0, rec1, rec2, rec3), (mid0, mid1, mid2, mid3), (far0, far1, far2, far3)
    mid_of, end_of, second = [], [], [[], [], [], []]

    def open_stream(n):
        from_partner(n)
        if n % 2 == 0:
            r = relay(lambda q, h: pown[n].at[2 * h:2 * h + 2, q], recs[n], rel_s, rel_r, x, *xn, base=6 * n)
        else:
            r = relay(lambda q, h: pown[n].at[q, 2 * h:2 * h + 2], recs[n], rel_s, rel_r, y, *yn, base=6 * n)
        mid_of.append((r[1], r[0]))
        end_of.append(r[2])

    def second_stage(n):
        mids[n][0:2], mids[n][2:4] = end_of[n]()
        for d in (2, 1, 3):
            if n % 2 == 0:
                src, to = mids[n].at[(y + d) % 4], col_of((y + d) % 4, x)
            else:
                src, to = mids[n].at[(x + d) % 4], col_of(y, (x + d) % 4)
            second[n].append(exchange(src, fars[n], far_s, far_r, d, to, n=3 * n))

    def close_stream(n):
        for cp in second[n]:
            cp.wait_recv()
        lo, hi = STREAMS[n]
        own_part = mids[n][y if n % 2 == 0 else x]
        ysum[:, lo:hi] = own_part + fars[n][0] + fars[n][1] + fars[n][2]

    arrived(0)
    to_partner(0)
    put(pown, 0, part(e, 0))
    arrived(1)
    to_partner(1)
    open_stream(0)
    put(pown, 1, part(e, 1))
    arrived(2)
    to_partner(2)
    open_stream(1)
    put(pown, 2, part(e, 2))
    mid_of[0][0]()
    open_stream(2)
    open_stream(3)
    mid_of[1][0]()
    second_stage(0)
    mid_of[2][0]()
    mid_of[3][0]()
    second_stage(1)
    second_stage(2)
    second_stage(3)
    def add(i, right, left):
        val = tmm(jnp.concatenate(right, axis=0), jnp.concatenate(left, axis=0))
        for side in range(2):
            phi[i, side] += val.reshape(4, 4, 2, 8, W)[:, :, side]

    def pair_terms(n):
        at = pl.ds(*SETS[n])
        cp = pltpu.make_async_remote_copy(
            src_ref=phi.at[at, 1 - e], dst_ref=qrec.at[at],
            send_sem=q_s.at[n], recv_sem=q_r.at[n], device_id=(z, partner), device_id_type=MESH)
        cp.start()
        return cp

    group_rec, group_far, group_mid = gr[0::3], gr[1::3], gr[2::3]
    ga_rec, ga_mid = group_rec[0], group_mid[0]

    def met(n):
        terms[n].wait_recv()
        at = slice(SETS[n][0], SETS[n][0] + SETS[n][1])
        qrec[at] += phi[at, e]

    def spots(n, first_stage):
        along_x = GROUPS[n][4] == first_stage
        out = [((x + d) % 4, col_of(y, (x + d) % 4)) if along_x else ((y + d) % 4, col_of((y + d) % 4, x))
               for d in range(4)]
        return out

    def slab(n, q):
        blk, nb, lo, hi, xfirst = GROUPS[n]
        at = pl.ds(blk, nb)
        return qrec.at[at, :, q, :, lo:hi] if xfirst else qrec.at[at, q, :, :, lo:hi]

    def open_direct(n):
        to = spots(n, True)
        return [exchange(slab(n, to[d][0]), group_rec[n], g_s, g_r, d, to[d][1], n=3 + 3 * n) for d in (2, 1, 3)]

    def second_group(n):
        to = spots(n, False)
        return [exchange(group_mid[n].at[:, to[d][0]], group_far[n], gf_s, gf_r, d, to[d][1], n=3 * n)
                for d in (2, 1, 3)]

    def open_last(n):
        to = spots(n, True)
        lo, hi, xfirst = GROUPS[n][2:]
        cps = []
        for d, flip in ((2, 0), (2, 1), (1, 0), (3, 0), (1, 1), (3, 1), (0, 1)):
            side = (e + flip) % 2
            src = phi.at[5, side, :, to[d][0], :, lo:hi] if xfirst else phi.at[5, side, to[d][0], :, :, lo:hi]
            at = 2 * d + flip - 1
            cp = pltpu.make_async_remote_copy(
                src_ref=src, dst_ref=group_rec[n].at[at],
                send_sem=last_s.at[7 * (n - 3) + at], recv_sem=last_r.at[7 * (n - 3) + at],
                device_id=(z, to[d][1] - e + side), device_id_type=MESH)
            cp.start()
            cps.append(cp)
        return cps

    def turn_last(n, cps):
        for cp in cps:
            cp.wait_recv()
        lo, hi, xfirst = GROUPS[n][2:]
        val = phi[5, e, :, x, :, lo:hi] if xfirst else phi[5, e, y, :, :, lo:hi]
        for at in range(7):
            val = val + group_rec[n][at]
        group_mid[n][0] = val
        return second_group(n)

    def turn_direct(n, cps):
        for cp in cps:
            cp.wait_recv()
        rec = group_rec[n]
        group_mid[n][...] = slab(n, x if GROUPS[n][4] else y)[...] + rec[0] + rec[1] + rec[2]
        return second_group(n)

    def close_group(n, cps):
        for cp in cps:
            cp.wait_recv()
        far = group_far[n]
        return group_mid[n][:, y if GROUPS[n][4] else x] + far[0] + far[1] + far[2]

    def pack(blk, val):
        for zz in range(16):
            for i in range(val.shape[0]):
                at = 16 * (blk + i)
                zsend[zz, :, at:at + 16] = val[i][:, 16 * zz:16 * zz + 16]

    gave = []

    def give(n, val):
        o_vm[n] = val
        cp = pltpu.make_async_copy(o_vm.at[n], o.at[n], o_sem.at[n])
        cp.start()
        gave.append(cp)

    terms = []
    close_stream(0)
    y1 = ysum[:, 0:W]
    a = mm(y1, c0)
    w = mm(y1, c1)
    u = mm(a, c2)
    add(0, [y1], [f1])
    add(1, [f2, -a], [y1, f1])
    add(2, [f3 - h, u - w], [y1, f1])
    terms.append(pair_terms(0))
    give(0, -y1)
    close_stream(1)
    y2 = (ysum[:, W:2 * W] - a) * keep2
    v = mm(y2, c2)
    add(3, [y2, -f2, a], [f2, a, b])
    add(4, [f3, -(w + v), g + h, -u], [y2, f2, a, b])
    terms.append(pair_terms(1))
    give(1, -y2)
    met(0)
    wide, wide_mid, wide_end = relay(
        lambda q, hh: qrec.at[0:3, 2 * hh:2 * hh + 2, q], ga_rec, g_s, g_r, x, *xn)
    for zz in range(16):
        zsend[zz, :, 96:128] = jnp.zeros((8, 32), F32)
    close_stream(2)
    close_stream(3)
    y3 = (ysum[:, 2 * W:3 * W] - w - v) * keep3
    add(5, [y3, h - f3, w - u, -f3, w + v, -(g + h), u], [f3, w, g, v, h, u, q_])
    firsts, lasts = {}, {}
    for n in (3, 4):
        firsts[n] = open_last(n)
    give(2, -y3)
    met(1)
    for n in (1, 2):
        firsts[n] = open_direct(n)
    wide_mid()
    ga_mid[:, 0:2], ga_mid[:, 2:4] = wide_end()
    lasts[0] = second_group(0)
    for n in (3, 4):
        lasts[n] = turn_last(n, firsts[n])
    for n in (1, 2):
        lasts[n] = turn_direct(n, firsts[n])
    pack(0, close_group(0, lasts[0]))
    for n, blk in ((1, 3), (3, 5)):
        left, right = close_group(n, lasts[n]), close_group(n + 1, lasts[n + 1])
        pack(blk, jnp.concatenate([left, right], axis=2))

    zc = []
    for d in (8, 7, 9, 6, 10, 5, 11, 4, 12, 3, 13, 2, 14, 1, 15):
        to = (z + d) % 16
        cp = pltpu.make_async_remote_copy(
            src_ref=zsend.at[to], dst_ref=zrec.at[d - 1], send_sem=z_s.at[d - 1], recv_sem=z_r.at[d - 1],
            device_id=(to, c), device_id_type=MESH)
        cp.start()
        zc.append(cp)
    for cp in zc:
        cp.wait_recv()
    tile = zsend[z]
    for d in range(15):
        tile = tile + zrec[d]
    ot[...] = tile

    for cp in gave:
        cp.wait()
    for way in (1, -1):
        for dist in range(1, REACH[way] + 1):
            for q in range(3):
                hop(z, dist - 1, 1, q, way).wait_send()
    for i in range(16):
        @pl.when((i * 2 + half) != c)
        def _():
            for q in range(3):
                plane_copy(i, q).wait_send()
    near = [cp for _, cps in mid_of for cp in cps]
    near += wide + [cp for n in firsts for cp in firsts[n]] + [cp for n in lasts for cp in lasts[n]]
    for cp in pair + near + second[0] + second[1] + second[2] + second[3] + terms + zc:
        cp.wait_send()


def hand_out(blocks, tile, o1, o2, o3, ot):
    o1[...] = blocks[0]
    o2[...] = blocks[1]
    o3[...] = blocks[2]
    for i, n in enumerate((0, 3, 5, 1, 2, 4)):
        ot[i] = tile[:, 16 * n:16 * n + 16]


def body(ancestor_inverse, panel_one, panel_two, panel_three, couplings, diag_terms, list_two, list_three):
    any_spec = pl.BlockSpec(memory_space=pl.ANY)
    vm = pl.BlockSpec(memory_space=pltpu.VMEM)
    dma = pltpu.SemaphoreType.DMA
    blocks, tile = pl.pallas_call(
        kernel,
        out_shape=(
            jax.ShapeDtypeStruct((3, ROWS, W), F32),
            jax.ShapeDtypeStruct((8, 128), F32),
        ),
        in_specs=[any_spec] * 6 + [vm] * 2,
        out_specs=(any_spec, vm),
        scratch_shapes=[
            pltpu.VMEM((1024, 512), F32),
            pltpu.VMEM((3, W, W), BF16),
            pltpu.VMEM((3, W, W), F32),
            pltpu.VMEM((16, 2, 32, 512), BF16),
            pltpu.VMEM((16, 2, 32, 512), BF16),
            pltpu.VMEM((16, 3, ROWS, W), BF16),
            pltpu.VMEM((3, 16, ROWS, W), BF16),
            *[[pltpu.VMEM((4, 4, ROWS, hi - lo), F32) for lo, hi in STREAMS]] * 3,
            *[pltpu.VMEM((6, 2, ROWS, hi - lo), F32) for lo, hi in STREAMS],
            *[pltpu.VMEM((3, ROWS, hi - lo), F32) for lo, hi in STREAMS],
            *[pltpu.VMEM((4, ROWS, hi - lo), F32) for lo, hi in STREAMS],
            pltpu.VMEM((ROWS, 768), F32),
            pltpu.VMEM((6, 2, 4, 4, 8, W), F32),
            pltpu.VMEM((5, 4, 4, 8, W), F32),
            pltpu.VMEM((16, 8, 128), F32),
            pltpu.VMEM((15, 8, 128), F32),
            [pltpu.VMEM(shape, F32) for n, (_, nb, lo, hi, _) in enumerate(GROUPS) for shape in (
                ((6, nb, 2, 8, hi - lo), (3, nb, 4, 8, hi - lo), (7, 4, 8, hi - lo))[min(2, (n + 1) // 2)], (3, nb, 8, hi - lo), (nb, 4, 8, hi - lo))],
            pltpu.VMEM((3, ROWS, W), F32),
            dma((6,)), dma((3,)), pltpu.SemaphoreType.REGULAR,
            dma((24,)), dma((24,)), dma((21,)), dma((21,)), dma((48,)), dma((48,)), dma((4,)), dma((4,)),
            dma((24,)), dma((24,)), dma((12,)), dma((12,)),
            dma((2,)), dma((2,)), dma((14,)), dma((14,)), dma((12,)), dma((12,)), dma((15,)), dma((15,)), dma((15,)), dma((15,)),
        ],
        compiler_params=pltpu.CompilerParams(
            collective_id=0, has_side_effects=True, vmem_limit_bytes=56 << 20
        ),
        name="chain_inverse",
    )(
        ancestor_inverse, panel_one, panel_two, panel_three, couplings, diag_terms,
        list_two.reshape(1, -1), list_three.reshape(1, -1),
    )
    *inverses, small = pl.pallas_call(
        hand_out,
        out_shape=(jax.ShapeDtypeStruct((ROWS, W), F32),) * 3 + (jax.ShapeDtypeStruct((6, 8, 16), F32),),
        in_specs=[vm] * 2,
        out_specs=(vm,) * 4,
        name="hand_out",
    )(blocks, tile)
    return (*inverses, jnp.swapaxes(small, 1, 2))


def solution(mesh):
    rows = P(("row", "col"), None)
    return jax.shard_map(
        body,
        mesh=mesh,
        in_specs=(P("row", "col"), rows, rows, rows, P(), P(), P(), P()),
        out_specs=(rows, rows, rows, P(None, "row", "col")),
        check_vma=False,
    )
```

```python
import functools

import jax
import jax.numpy as jnp
from jax import lax
from jax.experimental import pallas as pl
from jax.experimental.pallas import tpu as pltpu
from jax.sharding import PartitionSpec as P

MESH = pl.DeviceIdType.MESH
F32 = jnp.float32
BF16 = jnp.bfloat16
NZ, NK, W, ROWS = 16, 16, 256, 32
REACH = {1: 8, -1: 7}
GROUPS = (
    (0, 3, 0, 256, True), (3, 2, 0, 128, True), (3, 2, 128, 256, False), (5, 1, 0, 128, True), (5, 1, 128, 256, False),
)
SETS = ((0, 3), (3, 2), (5, 1))
STREAMS = ((0, 256), (256, 512), (512, 640), (640, 768))


def halves(v):
    hi = v.astype(BF16)
    return hi, (v - hi.astype(F32)).astype(BF16)


def mm(v, c):
    hi, lo = halves(v)
    return jnp.dot(hi, c, preferred_element_type=F32) + jnp.dot(lo, c, preferred_element_type=F32)


def turned_dot(a, b):
    return lax.dot_general(a, b, (((0,), (0,)), ((), ())), preferred_element_type=F32)


def tmc(v, c):
    hi, lo = halves(v)
    return turned_dot(hi, c) + turned_dot(lo, c)


def ctm(c, v):
    hi, lo = halves(v)
    return turned_dot(c, hi) + turned_dot(c, lo)


def tmm(a, b):
    ah, al = halves(a)
    bh, bl = halves(b)
    return turned_dot(jnp.concatenate([ah, al, ah], axis=0), jnp.concatenate([bh, bh, bl], axis=0))


def keep_of(lines, block):
    return jnp.max(jnp.where(lines == block, 1.0, 0.0).astype(F32))


def kernel(
    a_hbm, p1, p2, p3, coup_hbm, diag_hbm, l2, l3,
    o, ot,
    a_vm, coup, diag, ahi, alo, ring, fbuf, pown, ppar, prec,
    rec0, rec1, rec2, rec3, far0, far1, far2, far3, mid0, mid1, mid2, mid3, ysum,
    phi, qrec, zsend, zrec, gr,
    lsem, in_sem, up_s, up_r, dn_s, dn_r, f_s, f_r, pr_s, pr_r,
    rel_s, rel_r, far_s, far_r,
    q_s, q_r, g_s, g_r, gf_s, gf_r, z_s, z_r,
):
    z = lax.axis_index("row")
    c = lax.axis_index("col")
    e = c % 2
    k = c // 2
    y = k // 4
    x = k % 4
    half = y // 2
    partner = k * 2 + (1 - e)

    def col_of(yy, xx):
        return (yy * 4 + xx) * 2 + e

    own = []
    for i, p in enumerate((p1, p2, p3)):
        cp = pltpu.make_async_copy(p, ring.at[z, i], lsem.at[1 + i])
        cp.start()
        own.append(cp)
    acopy = pltpu.make_async_copy(a_hbm, a_vm, lsem.at[0])
    ccopy = pltpu.make_async_copy(coup_hbm, coup, lsem.at[4])
    dcopy = pltpu.make_async_copy(diag_hbm, diag, lsem.at[5])
    for cp in (acopy, ccopy, dcopy):
        cp.start()

    barrier = pltpu.get_barrier_semaphore()
    line = [partner]
    cross = []
    for d in (1, 2, 3):
        for ee in (0, 1):
            line.append((y * 4 + (x + d) % 4) * 2 + ee)
            cross.append(((y + d) % 4 * 4 + x) * 2 + ee)
    for to in line + cross:
        pl.semaphore_signal(barrier, inc=1, device_id=(z, to), device_id_type=MESH)
    for d in (1, 2, 14, 15):
        pl.semaphore_signal(barrier, inc=1, device_id=((z + d) % 16, c), device_id_type=MESH)
    for cp in own:
        cp.wait()
    pl.semaphore_wait(barrier, 17)
    for to in cross:
        pl.semaphore_signal(in_sem, inc=1, device_id=(z, to), device_id_type=MESH)

    slot = (k % 8) * 2 + e

    def hop(item, dist, step, q, way):
        send, recv = (up_s, up_r) if way > 0 else (dn_s, dn_r)
        part = ring.at[item, q]
        n = 3 * (dist + step - 1) + q
        return pltpu.make_async_remote_copy(
            src_ref=part, dst_ref=part, send_sem=send.at[n], recv_sem=recv.at[n],
            device_id=((z + 16 + way * step) % 16, c), device_id_type=MESH)

    def item_at(dist, way):
        return (z + 16 - way * dist) % 16

    def push(dist, q, way):
        for step in (2, 1):
            if dist + step <= REACH[way]:
                hop(item_at(dist, way), dist, step, q, way).start()

    def landed(dist, q, way):
        hop(item_at(dist, way), dist - 1, 1, q, way).wait_recv()

    def plane_copy(item, q):
        return pltpu.make_async_remote_copy(
            src_ref=ring.at[item, q], dst_ref=fbuf.at[q, slot],
            send_sem=f_s.at[3 * item + q], recv_sem=f_r.at[3 * slot + q],
            device_id=(z, item * 2 + half), device_id_type=MESH)

    def spread(item, q):
        mine = (item * 2 + half) == c

        @pl.when(mine)
        def _():
            pltpu.make_async_copy(ring.at[item, q], fbuf.at[q, slot], f_r.at[3 * slot + q]).start()

        @pl.when(jnp.logical_not(mine))
        def _():
            plane_copy(item, q).start()

    for q in range(3):
        for way in (1, -1):
            push(0, q, way)
    pl.semaphore_wait(in_sem, 6)
    for q in range(3):
        spread(z, q)
    def level(dist):
        for at in (dist, dist - 1):
            for q in range(3):
                for way in (1, -1):
                    if at <= REACH[way]:
                        landed(at, q, way)
                        if at == dist:
                            push(at, q, way)
                        spread(item_at(at, way), q)

    lines2 = l2[...]
    lines3 = l3[...]
    block = (z * 32 + c) // 8
    keep2 = keep_of(lines2, block)
    keep3 = keep_of(lines3, block)
    level(2)
    acopy.wait()

    @pl.loop(0, 16)
    def _(i):
        hi, lo = halves(a_vm[pl.ds(pl.multiple_of(i * 64, 64), 64), :])
        ahi[i] = hi.reshape(2, 32, 512)
        alo[i] = lo.reshape(2, 32, 512)

    level(4)
    ccopy.wait()
    dcopy.wait()
    c0, c1, c2 = coup[0], coup[1], coup[2]
    first = jnp.where((z == 0) & (c == 0), 1.0, 0.0).astype(F32)
    g1 = diag[0]
    h21 = -mm(g1, c0)
    g2 = diag[1] - ctm(c0, h21)
    level(6)
    h31 = -(mm(g1, c1) + mm(h21, c2))
    h32 = -(tmc(h21, c1) + mm(g2, c2))
    g3 = diag[2] - ctm(c1, h31) - ctm(c2, h32)
    for i, v in enumerate((g1, h21, h31, g2, h32, g3)):
        for side in range(2):
            phi[i, side] = (v.T * first).reshape(4, 4, 2, 8, W)[:, :, side]
    f1 = ring[z, 0].astype(F32)
    f2 = ring[z, 1].astype(F32) * keep2
    f3 = ring[z, 2].astype(F32) * keep3
    b = mm(f1, c0)
    g = mm(f1, c1)
    h = mm(f2, c2)
    q_ = mm(b, c2)
    level(8)

    def arrived(q):
        for i in range(16):
            pltpu.make_async_copy(ring.at[i, q], fbuf.at[q, i], f_r.at[3 * i + q]).wait()
        if q:
            lines = lines2 if q == 1 else lines3
            for j in range(2):
                s8 = slice(8 * j, 8 * j + 8)
                fbuf[q, s8] = (fbuf[q, s8].astype(F32) * keep_of(lines, 2 * c + j)).astype(BF16)

    def part(side, q):
        f = fbuf[q].reshape(512, W)
        out = jnp.dot(ahi[:, side].reshape(512, 512), f, preferred_element_type=F32)
        out = out + jnp.dot(alo[:, side].reshape(512, 512), f, preferred_element_type=F32)
        return out.reshape(4, 4, ROWS, W)

    def put(bufs, q, val):
        for n, (lo, hi) in enumerate(STREAMS):
            if q * W <= lo < (q + 1) * W:
                bufs[n][...] = val[:, :, :, lo - q * W:hi - q * W]

    pair = []

    def to_partner(q):
        put(ppar, q, part(1 - e, q))
        for n in ((0,), (1,), (2, 3))[q]:
            cp = pltpu.make_async_remote_copy(
                src_ref=ppar[n], dst_ref=prec[n],
                send_sem=pr_s.at[n], recv_sem=pr_r.at[n], device_id=(z, partner), device_id_type=MESH)
            cp.start()
            pair.append(cp)

    def from_partner(n):
        pair[n].wait_recv()
        pown[n][...] += prec[n][...]

    def exchange(src, rec, send, recv, d, to, n=0):
        cp = pltpu.make_async_remote_copy(
            src_ref=src, dst_ref=rec.at[d - 1], send_sem=send.at[n + d - 1], recv_sem=recv.at[n + d - 1],
            device_id=(z, to), device_id_type=MESH)
        cp.start()
        return cp

    def relay(view, rec, send, recv, p, right, left, base=0):
        def go(ref, n, to):
            cp = pltpu.make_async_remote_copy(
                src_ref=ref, dst_ref=rec.at[n], send_sem=send.at[base + n], recv_sem=recv.at[base + n],
                device_id=(z, to), device_id_type=MESH)
            cp.start()
            return cp

        far, after, before = (p + 2) % 4, (p + 1) % 4, (p + 3) % 4
        cps = [go(view(far, 0), 0, right), go(view(far, 1), 1, left),
               go(view(after, 1), 2, right), go(view(before, 0), 3, left)]

        def middle():
            for n, q, h, to in ((0, after, 0, right), (1, before, 1, left)):
                cps[n].wait_recv()
                ref = view(q, h)
                ref[...] += rec[n]
                cps.append(go(ref, 4 + n, to))

        def finish():
            for cp in cps[2:]:
                cp.wait_recv()
            return view(p, 0)[...] + rec[3] + rec[4], view(p, 1)[...] + rec[2] + rec[5]

        return cps, middle, finish

    xn, yn = [col_of(y, (x + d) % 4) for d in (1, 3)], [col_of((y + d) % 4, x) for d in (1, 3)]
    recs, mids, fars = (rec0, rec1, rec2, rec3), (mid0, mid1, mid2, mid3), (far0, far1, far2, far3)
    mid_of, end_of, second = [], [], [[], [], [], []]

    def open_stream(n):
        from_partner(n)
        if n % 2 == 0:
            r = relay(lambda q, h: pown[n].at[2 * h:2 * h + 2, q], recs[n], rel_s, rel_r, x, *xn, base=6 * n)
        else:
            r = relay(lambda q, h: pown[n].at[q, 2 * h:2 * h + 2], recs[n], rel_s, rel_r, y, *yn, base=6 * n)
        mid_of.append((r[1], r[0]))
        end_of.append(r[2])

    def second_stage(n):
        mids[n][0:2], mids[n][2:4] = end_of[n]()
        for d in (2, 1, 3):
            if n % 2 == 0:
                src, to = mids[n].at[(y + d) % 4], col_of((y + d) % 4, x)
            else:
                src, to = mids[n].at[(x + d) % 4], col_of(y, (x + d) % 4)
            second[n].append(exchange(src, fars[n], far_s, far_r, d, to, n=3 * n))

    def close_stream(n):
        for cp in second[n]:
            cp.wait_recv()
        lo, hi = STREAMS[n]
        own_part = mids[n][y if n % 2 == 0 else x]
        ysum[:, lo:hi] = own_part + fars[n][0] + fars[n][1] + fars[n][2]

    arrived(0)
    to_partner(0)
    put(pown, 0, part(e, 0))
    arrived(1)
    to_partner(1)
    open_stream(0)
    put(pown, 1, part(e, 1))
    arrived(2)
    to_partner(2)
    open_stream(1)
    put(pown, 2, part(e, 2))
    mid_of[0][0]()
    open_stream(2)
    open_stream(3)
    mid_of[1][0]()
    mid_of[2][0]()
    mid_of[3][0]()
    second_stage(0)
    second_stage(1)
    second_stage(2)
    second_stage(3)
    def add(i, right, left):
        val = tmm(jnp.concatenate(right, axis=0), jnp.concatenate(left, axis=0))
        for side in range(2):
            phi[i, side] += val.reshape(4, 4, 2, 8, W)[:, :, side]

    def pair_terms(n):
        at = pl.ds(*SETS[n])
        cp = pltpu.make_async_remote_copy(
            src_ref=phi.at[at, 1 - e], dst_ref=qrec.at[at],
            send_sem=q_s.at[n], recv_sem=q_r.at[n], device_id=(z, partner), device_id_type=MESH)
        cp.start()
        return cp

    group_rec, group_far, group_mid = gr[0::3], gr[1::3], gr[2::3]
    ga_rec, ga_mid = group_rec[0], group_mid[0]

    def met(n):
        terms[n].wait_recv()
        at = slice(SETS[n][0], SETS[n][0] + SETS[n][1])
        qrec[at] += phi[at, e]

    def spots(n, first_stage):
        along_x = GROUPS[n][4] == first_stage
        out = [((x + d) % 4, col_of(y, (x + d) % 4)) if along_x else ((y + d) % 4, col_of((y + d) % 4, x))
               for d in range(4)]
        return out

    def slab(n, q):
        blk, nb, lo, hi, xfirst = GROUPS[n]
        at = pl.ds(blk, nb)
        return qrec.at[at, :, q, :, lo:hi] if xfirst else qrec.at[at, q, :, :, lo:hi]

    def open_direct(n):
        to = spots(n, True)
        return [exchange(slab(n, to[d][0]), group_rec[n], g_s, g_r, d, to[d][1], n=3 + 3 * n) for d in (2, 1, 3)]

    def second_group(n):
        to = spots(n, False)
        return [exchange(group_mid[n].at[:, to[d][0]], group_far[n], gf_s, gf_r, d, to[d][1], n=3 * n)
                for d in (2, 1, 3)]

    def turn_direct(n, cps):
        for cp in cps:
            cp.wait_recv()
        rec = group_rec[n]
        group_mid[n][...] = slab(n, x if GROUPS[n][4] else y)[...] + rec[0] + rec[1] + rec[2]
        return second_group(n)

    def close_group(n, cps):
        for cp in cps:
            cp.wait_recv()
        far = group_far[n]
        return group_mid[n][:, y if GROUPS[n][4] else x] + far[0] + far[1] + far[2]

    def pack(blk, val):
        for zz in range(16):
            for i in range(val.shape[0]):
                at = 16 * (blk + i)
                zsend[zz, :, at:at + 16] = val[i][:, 16 * zz:16 * zz + 16]

    terms = []
    close_stream(0)
    y1 = ysum[:, 0:W]
    a = mm(y1, c0)
    w = mm(y1, c1)
    u = mm(a, c2)
    add(0, [y1], [f1])
    add(1, [f2, -a], [y1, f1])
    add(2, [f3 - h, u - w], [y1, f1])
    terms.append(pair_terms(0))
    o[0] = -y1
    close_stream(1)
    y2 = (ysum[:, W:2 * W] - a) * keep2
    v = mm(y2, c2)
    add(3, [y2, -f2, a], [f2, a, b])
    add(4, [f3, -(w + v), g + h, -u], [y2, f2, a, b])
    terms.append(pair_terms(1))
    o[1] = -y2
    met(0)
    wide, wide_mid, wide_end = relay(
        lambda q, hh: qrec.at[0:3, 2 * hh:2 * hh + 2, q], ga_rec, g_s, g_r, x, *xn)
    for zz in range(16):
        zsend[zz, :, 96:128] = jnp.zeros((8, 32), F32)
    close_stream(2)
    close_stream(3)
    y3 = (ysum[:, 2 * W:3 * W] - w - v) * keep3
    add(5, [y3, h - f3, w - u, -f3, w + v, -(g + h), u], [f3, w, g, v, h, u, q_])
    terms.append(pair_terms(2))
    o[2] = -y3
    met(1)
    firsts, lasts = {}, {}
    for n in (1, 2):
        firsts[n] = open_direct(n)
    wide_mid()
    met(2)
    for n in (3, 4):
        firsts[n] = open_direct(n)
    ga_mid[:, 0:2], ga_mid[:, 2:4] = wide_end()
    lasts[0] = second_group(0)
    for n in (1, 2, 3, 4):
        lasts[n] = turn_direct(n, firsts[n])
    pack(0, close_group(0, lasts[0]))
    for n, blk in ((1, 3), (3, 5)):
        left, right = close_group(n, lasts[n]), close_group(n + 1, lasts[n + 1])
        pack(blk, jnp.concatenate([left, right], axis=2))

    zc = []
    for d in (8, 7, 9, 6, 10, 5, 11, 4, 12, 3, 13, 2, 14, 1, 15):
        to = (z + d) % 16
        cp = pltpu.make_async_remote_copy(
            src_ref=zsend.at[to], dst_ref=zrec.at[d - 1], send_sem=z_s.at[d - 1], recv_sem=z_r.at[d - 1],
            device_id=(to, c), device_id_type=MESH)
        cp.start()
        zc.append(cp)
    for cp in zc:
        cp.wait_recv()
    tile = zsend[z]
    for d in range(15):
        tile = tile + zrec[d]
    ot[...] = tile

    for way in (1, -1):
        for dist in range(1, REACH[way] + 1):
            for q in range(3):
                hop(z, dist - 1, 1, q, way).wait_send()
    for i in range(16):
        @pl.when((i * 2 + half) != c)
        def _():
            for q in range(3):
                plane_copy(i, q).wait_send()
    near = [cp for _, cps in mid_of for cp in cps]
    near += wide + [cp for n in firsts for cp in firsts[n]] + [cp for n in lasts for cp in lasts[n]]
    for cp in pair + near + second[0] + second[1] + second[2] + second[3] + terms + zc:
        cp.wait_send()


def hand_out(blocks, tile, o1, o2, o3, ot):
    o1[...] = blocks[0]
    o2[...] = blocks[1]
    o3[...] = blocks[2]
    for i, n in enumerate((0, 3, 5, 1, 2, 4)):
        ot[i] = tile[:, 16 * n:16 * n + 16]


def body(ancestor_inverse, panel_one, panel_two, panel_three, couplings, diag_terms, list_two, list_three):
    any_spec = pl.BlockSpec(memory_space=pl.ANY)
    vm = pl.BlockSpec(memory_space=pltpu.VMEM)
    dma = pltpu.SemaphoreType.DMA
    blocks, tile = pl.pallas_call(
        kernel,
        out_shape=(
            jax.ShapeDtypeStruct((3, ROWS, W), F32),
            jax.ShapeDtypeStruct((8, 128), F32),
        ),
        in_specs=[any_spec] * 6 + [vm] * 2,
        out_specs=(vm,) * 2,
        scratch_shapes=[
            pltpu.VMEM((1024, 512), F32),
            pltpu.VMEM((3, W, W), BF16),
            pltpu.VMEM((3, W, W), F32),
            pltpu.VMEM((16, 2, 32, 512), BF16),
            pltpu.VMEM((16, 2, 32, 512), BF16),
            pltpu.VMEM((16, 3, ROWS, W), BF16),
            pltpu.VMEM((3, 16, ROWS, W), BF16),
            *[[pltpu.VMEM((4, 4, ROWS, hi - lo), F32) for lo, hi in STREAMS]] * 3,
            *[pltpu.VMEM((6, 2, ROWS, hi - lo), F32) for lo, hi in STREAMS],
            *[pltpu.VMEM((3, ROWS, hi - lo), F32) for lo, hi in STREAMS],
            *[pltpu.VMEM((4, ROWS, hi - lo), F32) for lo, hi in STREAMS],
            pltpu.VMEM((ROWS, 768), F32),
            pltpu.VMEM((6, 2, 4, 4, 8, W), F32),
            pltpu.VMEM((6, 4, 4, 8, W), F32),
            pltpu.VMEM((16, 8, 128), F32),
            pltpu.VMEM((15, 8, 128), F32),
            [pltpu.VMEM(shape, F32) for n, (_, nb, lo, hi, _) in enumerate(GROUPS) for shape in (
                (3, nb, 4, 8, hi - lo) if n else (6, nb, 2, 8, hi - lo), (3, nb, 8, hi - lo), (nb, 4, 8, hi - lo))],
            dma((6,)), pltpu.SemaphoreType.REGULAR,
            dma((24,)), dma((24,)), dma((21,)), dma((21,)), dma((48,)), dma((48,)), dma((4,)), dma((4,)),
            dma((24,)), dma((24,)), dma((12,)), dma((12,)),
            dma((3,)), dma((3,)), dma((18,)), dma((18,)), dma((15,)), dma((15,)), dma((15,)), dma((15,)),
        ],
        compiler_params=pltpu.CompilerParams(
            collective_id=0, has_side_effects=True, vmem_limit_bytes=56 << 20
        ),
        name="chain_inverse",
    )(
        ancestor_inverse, panel_one, panel_two, panel_three, couplings, diag_terms,
        list_two.reshape(1, -1), list_three.reshape(1, -1),
    )
    *inverses, small = pl.pallas_call(
        hand_out,
        out_shape=(jax.ShapeDtypeStruct((ROWS, W), F32),) * 3 + (jax.ShapeDtypeStruct((6, 8, 16), F32),),
        in_specs=[vm] * 2,
        out_specs=(vm,) * 4,
        name="hand_out",
    )(blocks, tile)
    return (*inverses, jnp.swapaxes(small, 1, 2))


def solution(mesh):
    rows = P(("row", "col"), None)
    return jax.shard_map(
        body,
        mesh=mesh,
        in_specs=(P("row", "col"), rows, rows, rows, P(), P(), P(), P()),
        out_specs=(rows, rows, rows, P(None, "row", "col")),
        check_vma=False,
    )
```

```python
import functools

import jax
import jax.numpy as jnp
from jax import lax
from jax.experimental import pallas as pl
from jax.experimental.pallas import tpu as pltpu
from jax.sharding import PartitionSpec as P

MESH = pl.DeviceIdType.MESH
F32 = jnp.float32
BF16 = jnp.bfloat16
NZ, NK, W, ROWS = 16, 16, 256, 32
REACH = {1: 8, -1: 7}
GROUPS = (
    (0, 3, 0, 256, True), (3, 2, 0, 128, True), (3, 2, 128, 256, False), (5, 1, 0, 128, True), (5, 1, 128, 256, False),
)
SETS = ((0, 3), (3, 2), (5, 1))
STREAMS = ((0, 256), (256, 512), (512, 640), (640, 768))


def halves(v):
    hi = v.astype(BF16)
    return hi, (v - hi.astype(F32)).astype(BF16)


def mm(v, c):
    hi, lo = halves(v)
    return jnp.dot(hi, c, preferred_element_type=F32) + jnp.dot(lo, c, preferred_element_type=F32)


def turned_dot(a, b):
    return lax.dot_general(a, b, (((0,), (0,)), ((), ())), preferred_element_type=F32)


def tmc(v, c):
    hi, lo = halves(v)
    return turned_dot(hi, c) + turned_dot(lo, c)


def ctm(c, v):
    hi, lo = halves(v)
    return turned_dot(c, hi) + turned_dot(c, lo)


def tmm(a, b):
    ah, al = halves(a)
    bh, bl = halves(b)
    return turned_dot(jnp.concatenate([ah, al, ah], axis=0), jnp.concatenate([bh, bh, bl], axis=0))


def keep_of(lines, block):
    return jnp.max(jnp.where(lines == block, 1.0, 0.0).astype(F32))


def kernel(
    a_hbm, p1, p2, p3, coup_hbm, diag_hbm, l2, l3,
    o, ot,
    a_vm, coup, diag, ahi, alo, ring, fbuf, pown, ppar, prec,
    rec0, rec1, rec2, rec3, far0, far1, far2, far3, mid0, mid1, mid2, mid3, ysum,
    phi, qrec, zsend, zrec, gr, o_vm,
    lsem, o_sem, in_sem, up_s, up_r, dn_s, dn_r, f_s, f_r, pr_s, pr_r,
    rel_s, rel_r, far_s, far_r,
    q_s, q_r, g_s, g_r, gf_s, gf_r, z_s, z_r,
):
    z = lax.axis_index("row")
    c = lax.axis_index("col")
    e = c % 2
    k = c // 2
    y = k // 4
    x = k % 4
    half = y // 2
    partner = k * 2 + (1 - e)

    def col_of(yy, xx):
        return (yy * 4 + xx) * 2 + e

    own = []
    for i, p in enumerate((p1, p2, p3)):
        cp = pltpu.make_async_copy(p, ring.at[z, i], lsem.at[1 + i])
        cp.start()
        own.append(cp)
    acopy = pltpu.make_async_copy(a_hbm, a_vm, lsem.at[0])
    ccopy = pltpu.make_async_copy(coup_hbm, coup, lsem.at[4])
    dcopy = pltpu.make_async_copy(diag_hbm, diag, lsem.at[5])
    for cp in (acopy, ccopy, dcopy):
        cp.start()

    barrier = pltpu.get_barrier_semaphore()
    line = [partner]
    cross = []
    for d in (1, 2, 3):
        for ee in (0, 1):
            line.append((y * 4 + (x + d) % 4) * 2 + ee)
            cross.append(((y + d) % 4 * 4 + x) * 2 + ee)
    for to in line + cross:
        pl.semaphore_signal(barrier, inc=1, device_id=(z, to), device_id_type=MESH)
    for d in (1, 2, 14, 15):
        pl.semaphore_signal(barrier, inc=1, device_id=((z + d) % 16, c), device_id_type=MESH)
    for cp in own:
        cp.wait()
    pl.semaphore_wait(barrier, 17)
    for to in cross:
        pl.semaphore_signal(in_sem, inc=1, device_id=(z, to), device_id_type=MESH)

    slot = (k % 8) * 2 + e

    def hop(item, dist, step, q, way):
        send, recv = (up_s, up_r) if way > 0 else (dn_s, dn_r)
        part = ring.at[item, q]
        n = 3 * (dist + step - 1) + q
        return pltpu.make_async_remote_copy(
            src_ref=part, dst_ref=part, send_sem=send.at[n], recv_sem=recv.at[n],
            device_id=((z + 16 + way * step) % 16, c), device_id_type=MESH)

    def item_at(dist, way):
        return (z + 16 - way * dist) % 16

    def push(dist, q, way):
        for step in (2, 1):
            if dist + step <= REACH[way]:
                hop(item_at(dist, way), dist, step, q, way).start()

    def landed(dist, q, way):
        hop(item_at(dist, way), dist - 1, 1, q, way).wait_recv()

    def plane_copy(item, q):
        return pltpu.make_async_remote_copy(
            src_ref=ring.at[item, q], dst_ref=fbuf.at[q, slot],
            send_sem=f_s.at[3 * item + q], recv_sem=f_r.at[3 * slot + q],
            device_id=(z, item * 2 + half), device_id_type=MESH)

    def spread(item, q):
        mine = (item * 2 + half) == c

        @pl.when(mine)
        def _():
            pltpu.make_async_copy(ring.at[item, q], fbuf.at[q, slot], f_r.at[3 * slot + q]).start()

        @pl.when(jnp.logical_not(mine))
        def _():
            plane_copy(item, q).start()

    for q in range(3):
        for way in (1, -1):
            push(0, q, way)
    pl.semaphore_wait(in_sem, 6)
    for q in range(3):
        spread(z, q)
    def level(dist):
        for at in (dist, dist - 1):
            for q in range(3):
                for way in (1, -1):
                    if at <= REACH[way]:
                        landed(at, q, way)
                        if at == dist:
                            push(at, q, way)
                        spread(item_at(at, way), q)

    lines2 = l2[...]
    lines3 = l3[...]
    block = (z * 32 + c) // 8
    keep2 = keep_of(lines2, block)
    keep3 = keep_of(lines3, block)
    level(2)
    acopy.wait()

    @pl.loop(0, 16)
    def _(i):
        hi, lo = halves(a_vm[pl.ds(pl.multiple_of(i * 64, 64), 64), :])
        ahi[i] = hi.reshape(2, 32, 512)
        alo[i] = lo.reshape(2, 32, 512)

    level(4)
    ccopy.wait()
    dcopy.wait()
    c0, c1, c2 = coup[0], coup[1], coup[2]
    first = jnp.where((z == 0) & (c == 0), 1.0, 0.0).astype(F32)
    g1 = diag[0]
    h21 = -mm(g1, c0)
    g2 = diag[1] - ctm(c0, h21)
    level(6)
    h31 = -(mm(g1, c1) + mm(h21, c2))
    h32 = -(tmc(h21, c1) + mm(g2, c2))
    g3 = diag[2] - ctm(c1, h31) - ctm(c2, h32)
    for i, v in enumerate((g1, h21, h31, g2, h32, g3)):
        for side in range(2):
            phi[i, side] = (v.T * first).reshape(4, 4, 2, 8, W)[:, :, side]
    f1 = ring[z, 0].astype(F32)
    f2 = ring[z, 1].astype(F32) * keep2
    f3 = ring[z, 2].astype(F32) * keep3
    b = mm(f1, c0)
    g = mm(f1, c1)
    h = mm(f2, c2)
    q_ = mm(b, c2)
    level(8)

    def arrived(q):
        for i in range(16):
            pltpu.make_async_copy(ring.at[i, q], fbuf.at[q, i], f_r.at[3 * i + q]).wait()
        if q:
            lines = lines2 if q == 1 else lines3
            for j in range(2):
                s8 = slice(8 * j, 8 * j + 8)
                fbuf[q, s8] = (fbuf[q, s8].astype(F32) * keep_of(lines, 2 * c + j)).astype(BF16)

    def part(side, q):
        f = fbuf[q].reshape(512, W)
        out = jnp.dot(ahi[:, side].reshape(512, 512), f, preferred_element_type=F32)
        out = out + jnp.dot(alo[:, side].reshape(512, 512), f, preferred_element_type=F32)
        return out.reshape(4, 4, ROWS, W)

    def put(bufs, q, val):
        for n, (lo, hi) in enumerate(STREAMS):
            if q * W <= lo < (q + 1) * W:
                bufs[n][...] = val[:, :, :, lo - q * W:hi - q * W]

    pair = []

    def to_partner(q):
        put(ppar, q, part(1 - e, q))
        for n in ((0,), (1,), (2, 3))[q]:
            cp = pltpu.make_async_remote_copy(
                src_ref=ppar[n], dst_ref=prec[n],
                send_sem=pr_s.at[n], recv_sem=pr_r.at[n], device_id=(z, partner), device_id_type=MESH)
            cp.start()
            pair.append(cp)

    def from_partner(n):
        pair[n].wait_recv()
        pown[n][...] += prec[n][...]

    def exchange(src, rec, send, recv, d, to, n=0):
        cp = pltpu.make_async_remote_copy(
            src_ref=src, dst_ref=rec.at[d - 1], send_sem=send.at[n + d - 1], recv_sem=recv.at[n + d - 1],
            device_id=(z, to), device_id_type=MESH)
        cp.start()
        return cp

    def relay(view, rec, send, recv, p, right, left, base=0):
        def go(ref, n, to):
            cp = pltpu.make_async_remote_copy(
                src_ref=ref, dst_ref=rec.at[n], send_sem=send.at[base + n], recv_sem=recv.at[base + n],
                device_id=(z, to), device_id_type=MESH)
            cp.start()
            return cp

        far, after, before = (p + 2) % 4, (p + 1) % 4, (p + 3) % 4
        cps = [go(view(far, 0), 0, right), go(view(far, 1), 1, left),
               go(view(after, 1), 2, right), go(view(before, 0), 3, left)]

        def middle():
            for n, q, h, to in ((0, after, 0, right), (1, before, 1, left)):
                cps[n].wait_recv()
                ref = view(q, h)
                ref[...] += rec[n]
                cps.append(go(ref, 4 + n, to))

        def finish():
            for cp in cps[2:]:
                cp.wait_recv()
            return view(p, 0)[...] + rec[3] + rec[4], view(p, 1)[...] + rec[2] + rec[5]

        return cps, middle, finish

    xn, yn = [col_of(y, (x + d) % 4) for d in (1, 3)], [col_of((y + d) % 4, x) for d in (1, 3)]
    recs, mids, fars = (rec0, rec1, rec2, rec3), (mid0, mid1, mid2, mid3), (far0, far1, far2, far3)
    mid_of, end_of, second = [], [], [[], [], [], []]

    def open_stream(n):
        from_partner(n)
        if n % 2 == 0:
            r = relay(lambda q, h: pown[n].at[2 * h:2 * h + 2, q], recs[n], rel_s, rel_r, x, *xn, base=6 * n)
        else:
            r = relay(lambda q, h: pown[n].at[q, 2 * h:2 * h + 2], recs[n], rel_s, rel_r, y, *yn, base=6 * n)
        mid_of.append((r[1], r[0]))
        end_of.append(r[2])

    def second_stage(n):
        mids[n][0:2], mids[n][2:4] = end_of[n]()
        for d in (2, 1, 3):
            if n % 2 == 0:
                src, to = mids[n].at[(y + d) % 4], col_of((y + d) % 4, x)
            else:
                src, to = mids[n].at[(x + d) % 4], col_of(y, (x + d) % 4)
            second[n].append(exchange(src, fars[n], far_s, far_r, d, to, n=3 * n))

    def close_stream(n):
        for cp in second[n]:
            cp.wait_recv()
        lo, hi = STREAMS[n]
        own_part = mids[n][y if n % 2 == 0 else x]
        ysum[:, lo:hi] = own_part + fars[n][0] + fars[n][1] + fars[n][2]

    arrived(0)
    to_partner(0)
    put(pown, 0, part(e, 0))
    arrived(1)
    to_partner(1)
    open_stream(0)
    put(pown, 1, part(e, 1))
    arrived(2)
    to_partner(2)
    open_stream(1)
    put(pown, 2, part(e, 2))
    mid_of[0][0]()
    open_stream(2)
    open_stream(3)
    mid_of[1][0]()
    second_stage(0)
    mid_of[2][0]()
    mid_of[3][0]()
    second_stage(1)
    second_stage(2)
    second_stage(3)
    def add(i, right, left):
        val = tmm(jnp.concatenate(right, axis=0), jnp.concatenate(left, axis=0))
        for side in range(2):
            phi[i, side] += val.reshape(4, 4, 2, 8, W)[:, :, side]

    def pair_terms(n):
        at = pl.ds(*SETS[n])
        cp = pltpu.make_async_remote_copy(
            src_ref=phi.at[at, 1 - e], dst_ref=qrec.at[at],
            send_sem=q_s.at[n], recv_sem=q_r.at[n], device_id=(z, partner), device_id_type=MESH)
        cp.start()
        return cp

    group_rec, group_far, group_mid = gr[0::3], gr[1::3], gr[2::3]
    ga_rec, ga_mid = group_rec[0], group_mid[0]

    def met(n):
        terms[n].wait_recv()
        at = slice(SETS[n][0], SETS[n][0] + SETS[n][1])
        qrec[at] += phi[at, e]

    def spots(n, first_stage):
        along_x = GROUPS[n][4] == first_stage
        out = [((x + d) % 4, col_of(y, (x + d) % 4)) if along_x else ((y + d) % 4, col_of((y + d) % 4, x))
               for d in range(4)]
        return out

    def slab(n, q):
        blk, nb, lo, hi, xfirst = GROUPS[n]
        at = pl.ds(blk, nb)
        return qrec.at[at, :, q, :, lo:hi] if xfirst else qrec.at[at, q, :, :, lo:hi]

    def open_direct(n):
        to = spots(n, True)
        return [exchange(slab(n, to[d][0]), group_rec[n], g_s, g_r, d, to[d][1], n=3 + 3 * n) for d in (2, 1, 3)]

    def second_group(n):
        to = spots(n, False)
        return [exchange(group_mid[n].at[:, to[d][0]], group_far[n], gf_s, gf_r, d, to[d][1], n=3 * n)
                for d in (2, 1, 3)]

    def turn_direct(n, cps):
        for cp in cps:
            cp.wait_recv()
        rec = group_rec[n]
        group_mid[n][...] = slab(n, x if GROUPS[n][4] else y)[...] + rec[0] + rec[1] + rec[2]
        return second_group(n)

    def close_group(n, cps):
        for cp in cps:
            cp.wait_recv()
        far = group_far[n]
        return group_mid[n][:, y if GROUPS[n][4] else x] + far[0] + far[1] + far[2]

    def pack(blk, val):
        for zz in range(16):
            for i in range(val.shape[0]):
                at = 16 * (blk + i)
                zsend[zz, :, at:at + 16] = val[i][:, 16 * zz:16 * zz + 16]

    gave = []

    def give(n, val):
        o_vm[n] = val
        cp = pltpu.make_async_copy(o_vm.at[n], o.at[n], o_sem.at[n])
        cp.start()
        gave.append(cp)

    terms = []
    close_stream(0)
    y1 = ysum[:, 0:W]
    a = mm(y1, c0)
    w = mm(y1, c1)
    u = mm(a, c2)
    add(0, [y1], [f1])
    add(1, [f2, -a], [y1, f1])
    add(2, [f3 - h, u - w], [y1, f1])
    terms.append(pair_terms(0))
    give(0, -y1)
    close_stream(1)
    y2 = (ysum[:, W:2 * W] - a) * keep2
    v = mm(y2, c2)
    add(3, [y2, -f2, a], [f2, a, b])
    add(4, [f3, -(w + v), g + h, -u], [y2, f2, a, b])
    terms.append(pair_terms(1))
    give(1, -y2)
    met(0)
    wide, wide_mid, wide_end = relay(
        lambda q, hh: qrec.at[0:3, 2 * hh:2 * hh + 2, q], ga_rec, g_s, g_r, x, *xn)
    for zz in range(16):
        zsend[zz, :, 96:128] = jnp.zeros((8, 32), F32)
    close_stream(2)
    close_stream(3)
    y3 = (ysum[:, 2 * W:3 * W] - w - v) * keep3
    add(5, [y3, h - f3, w - u, -f3, w + v, -(g + h), u], [f3, w, g, v, h, u, q_])
    terms.append(pair_terms(2))
    give(2, -y3)
    met(1)
    firsts, lasts = {}, {}
    for n in (1, 2):
        firsts[n] = open_direct(n)
    wide_mid()
    met(2)
    for n in (3, 4):
        firsts[n] = open_direct(n)
    ga_mid[:, 0:2], ga_mid[:, 2:4] = wide_end()
    lasts[0] = second_group(0)
    for n in (1, 2, 3, 4):
        lasts[n] = turn_direct(n, firsts[n])
    pack(0, close_group(0, lasts[0]))
    for n, blk in ((1, 3), (3, 5)):
        left, right = close_group(n, lasts[n]), close_group(n + 1, lasts[n + 1])
        pack(blk, jnp.concatenate([left, right], axis=2))

    zc = []
    for d in (8, 7, 9, 6, 10, 5, 11, 4, 12, 3, 13, 2, 14, 1, 15):
        to = (z + d) % 16
        cp = pltpu.make_async_remote_copy(
            src_ref=zsend.at[to], dst_ref=zrec.at[d - 1], send_sem=z_s.at[d - 1], recv_sem=z_r.at[d - 1],
            device_id=(to, c), device_id_type=MESH)
        cp.start()
        zc.append(cp)
    for cp in zc:
        cp.wait_recv()
    tile = zsend[z]
    for d in range(15):
        tile = tile + zrec[d]
    ot[...] = tile

    for cp in gave:
        cp.wait()
    for way in (1, -1):
        for dist in range(1, REACH[way] + 1):
            for q in range(3):
                hop(z, dist - 1, 1, q, way).wait_send()
    for i in range(16):
        @pl.when((i * 2 + half) != c)
        def _():
            for q in range(3):
                plane_copy(i, q).wait_send()
    near = [cp for _, cps in mid_of for cp in cps]
    near += wide + [cp for n in firsts for cp in firsts[n]] + [cp for n in lasts for cp in lasts[n]]
    for cp in pair + near + second[0] + second[1] + second[2] + second[3] + terms + zc:
        cp.wait_send()


def hand_out(blocks, tile, o1, o2, o3, ot):
    o1[...] = blocks[0]
    o2[...] = blocks[1]
    o3[...] = blocks[2]
    for i, n in enumerate((0, 3, 5, 1, 2, 4)):
        ot[i] = tile[:, 16 * n:16 * n + 16]


def body(ancestor_inverse, panel_one, panel_two, panel_three, couplings, diag_terms, list_two, list_three):
    any_spec = pl.BlockSpec(memory_space=pl.ANY)
    vm = pl.BlockSpec(memory_space=pltpu.VMEM)
    dma = pltpu.SemaphoreType.DMA
    blocks, tile = pl.pallas_call(
        kernel,
        out_shape=(
            jax.ShapeDtypeStruct((3, ROWS, W), F32),
            jax.ShapeDtypeStruct((8, 128), F32),
        ),
        in_specs=[any_spec] * 6 + [vm] * 2,
        out_specs=(any_spec, vm),
        scratch_shapes=[
            pltpu.VMEM((1024, 512), F32),
            pltpu.VMEM((3, W, W), BF16),
            pltpu.VMEM((3, W, W), F32),
            pltpu.VMEM((16, 2, 32, 512), BF16),
            pltpu.VMEM((16, 2, 32, 512), BF16),
            pltpu.VMEM((16, 3, ROWS, W), BF16),
            pltpu.VMEM((3, 16, ROWS, W), BF16),
            *[[pltpu.VMEM((4, 4, ROWS, hi - lo), F32) for lo, hi in STREAMS]] * 3,
            *[pltpu.VMEM((6, 2, ROWS, hi - lo), F32) for lo, hi in STREAMS],
            *[pltpu.VMEM((3, ROWS, hi - lo), F32) for lo, hi in STREAMS],
            *[pltpu.VMEM((4, ROWS, hi - lo), F32) for lo, hi in STREAMS],
            pltpu.VMEM((ROWS, 768), F32),
            pltpu.VMEM((6, 2, 4, 4, 8, W), F32),
            pltpu.VMEM((6, 4, 4, 8, W), F32),
            pltpu.VMEM((16, 8, 128), F32),
            pltpu.VMEM((15, 8, 128), F32),
            [pltpu.VMEM(shape, F32) for n, (_, nb, lo, hi, _) in enumerate(GROUPS) for shape in (
                (3, nb, 4, 8, hi - lo) if n else (6, nb, 2, 8, hi - lo), (3, nb, 8, hi - lo), (nb, 4, 8, hi - lo))],
            pltpu.VMEM((3, ROWS, W), F32),
            dma((6,)), dma((3,)), pltpu.SemaphoreType.REGULAR,
            dma((24,)), dma((24,)), dma((21,)), dma((21,)), dma((48,)), dma((48,)), dma((4,)), dma((4,)),
            dma((24,)), dma((24,)), dma((12,)), dma((12,)),
            dma((3,)), dma((3,)), dma((18,)), dma((18,)), dma((15,)), dma((15,)), dma((15,)), dma((15,)),
        ],
        compiler_params=pltpu.CompilerParams(
            collective_id=0, has_side_effects=True, vmem_limit_bytes=56 << 20
        ),
        name="chain_inverse",
    )(
        ancestor_inverse, panel_one, panel_two, panel_three, couplings, diag_terms,
        list_two.reshape(1, -1), list_three.reshape(1, -1),
    )
    *inverses, small = pl.pallas_call(
        hand_out,
        out_shape=(jax.ShapeDtypeStruct((ROWS, W), F32),) * 3 + (jax.ShapeDtypeStruct((6, 8, 16), F32),),
        in_specs=[vm] * 2,
        out_specs=(vm,) * 4,
        name="hand_out",
    )(blocks, tile)
    return (*inverses, jnp.swapaxes(small, 1, 2))


def solution(mesh):
    rows = P(("row", "col"), None)
    return jax.shard_map(
        body,
        mesh=mesh,
        in_specs=(P("row", "col"), rows, rows, rows, P(), P(), P(), P()),
        out_specs=(rows, rows, rows, P(None, "row", "col")),
        check_vma=False,
    )
```
